256 devices in a mesh: section: 4 (over y_lo, core), seq: 16 (over y_hi, z), expert: 4 (over x).
Axes of the slice: x: 4, y: 4 (y_hi: 2, y_lo: 2; y = y_hi * 2 + y_lo), z: 8, core: 2. Of those that a mesh axis runs over, the one named last changes fastest.
Arguments:
- queries: bfloat16 [16, 1536, 4096], P(('section', 'expert'), 'seq'), may hold values from -112 to 112
- dec_state: bfloat16 [16, 1536, 4096], P(('section', 'expert'), 'seq'), may hold values from -6 to 6
- enc_kv: bfloat16 [2, 16, 2560, 1024], P(None, ('section', 'expert'), 'seq'), may hold values from -15 to 15
- band_start: int32 [16, 16], P(('section', 'expert'), 'seq'), may hold values from 0 to 2432, as said below
- norm_gain: float32 [4096], replicated, may hold values from 0.5 to 1.5
- route_ids: int32 [16, 1536, 1], P(('section', 'expert'), 'seq'), may hold values from 0 to 31; in each aligned block of 96 rows (0 to 95, 96 to 191, ..., all dimensions but the last counted through in order) at most 3 rows name the same one
- keep: int32 [16, 1536], P(('section', 'expert'), 'seq'), may hold values 0 or 1
- route_prob: float32 [16, 1536], P(('section', 'expert'), 'seq'), may hold values from 0.25 to 1
- w_in: bfloat16 [32, 5120, 4096], P('seq', ('section', 'expert')), may hold values from -0.09375 to 0.09375
- w_out: bfloat16 [32, 5120, 4096], P('seq', ('section', 'expert')), may hold values from -0.078125 to 0.078125
Outputs:
- mixed: bfloat16 [16, 1536, 4096], P(('section', 'expert'), 'seq')
The draws below stay inside these ranges and needn't reach their ends.
Inputs may be any that keep to these rules, and one draw needn't show every extreme that they name: `band_start`: block q's band lies within encoder frames (q - 1) * 160 to (q + 2) * 160 - 1. `route_ids`: among the tokens of one device no expert is named more than 3 times.
All inputs are finite; a program needn't handle non-finite values. No bound on the sum of `keep` on one device may be relied on, other than what follows from the above.
Results may differ from the reference program's by a relative error of at most 0.011.
Values may be sent and summed in bfloat16 or wider, within the bound.
A program may use at most 128 MiB of HBM per device.

```python
import math
import jax
import jax.numpy as jnp
import numpy as np
from jax import lax

D = 4096
HEADS = 32
KV_HEADS = 8
DH = 128
FF = 5120
WIN = 128
FR_DEV = 160
TOK_DEV = 96
UTT_SECTION = 4
UTT = 16
FRAMES = 2560
TOKENS = 1536
EXPERTS = 32
CAP = 3
GROUP = 16
FS = 320
N_SEQ = 16


def band_offsets(key):
    blocks = jnp.arange(N_SEQ, dtype=jnp.int32)[None, :]
    utterances = jnp.arange(UTT, dtype=jnp.int32)[:, None]
    jitter = jax.random.randint(jax.random.fold_in(key, 11), (UTT, N_SEQ), -FR_DEV, 2 * FR_DEV - WIN + 1, dtype=jnp.int32)
    starts = jnp.clip(blocks * FR_DEV + jitter, 0, FRAMES - WIN)
    starts = jnp.where((utterances == 0) & (blocks == 0), 0, starts)
    starts = jnp.where((utterances == UTT - 1) & (blocks == N_SEQ - 1), FRAMES - WIN, starts)
    return starts.astype(jnp.int32)


def key_values(key):
    keys_raw = jax.random.normal(jax.random.fold_in(key, 22), (UTT, FRAMES, KV_HEADS * DH), jnp.float32)
    keys_raw = jnp.clip(keys_raw, -6.0, 6.0)
    values_raw = jnp.clip(2.5 * jax.random.normal(jax.random.fold_in(key, 24), (UTT, FRAMES, KV_HEADS * DH), jnp.float32), -15.0, 15.0)
    return (keys_raw, values_raw)


def draw_band_start(key, part):
    return band_offsets(key)


def draw_enc_kv(key, part):
    keys_raw, values_raw = key_values(key)
    return jnp.stack([keys_raw, values_raw]).astype(jnp.bfloat16)


def draw_queries(key, part):
    drawn = jnp.clip(jax.random.normal(jax.random.fold_in(key, 31), (UTT, TOKENS, D), jnp.float32), -6.0, 6.0)
    return drawn.astype(jnp.bfloat16)


def set_ends(drawn, stream_key, low, top_value):
    spot = [jax.random.randint(jax.random.fold_in(stream_key, axis), (), 0, length) for axis, length in enumerate(drawn.shape)]
    widest = drawn.shape.index(max(drawn.shape))
    neighbour = spot[:widest] + [(spot[widest] + 1) % drawn.shape[widest]] + spot[widest + 1:]
    return drawn.at[tuple(spot)].set(low).at[tuple(neighbour)].set(top_value)


def block_levels(stream_key, extent, cuts, low, largest):
    factor_of, own = 1.0, jax.random.fold_in(stream_key, 6)
    for axis_at, shards_of in cuts:
        draws = jnp.exp(jax.random.uniform(jax.random.fold_in(own, axis_at), (shards_of,), jnp.float32, low / len(cuts), largest / len(cuts)))
        factor_of = factor_of * jnp.repeat(draws, extent[axis_at] // shards_of).reshape([-1 if axis == axis_at else 1 for axis in range(len(extent))])
    return factor_of


def deal_out(stream_key, own, number, rows, count, top, most, slope):
    sequence = jax.random.permutation(stream_key, count)
    packed, common = portions_of(count, rows * top, most, slope, True), portions_of(count, rows * top, most, slope, False)
    places = jnp.arange(count)

    def named(lengths, turn):
        used = int((lengths > 0).sum())
        fixed = max(1, used // 4)
        shifted = fixed + (places - fixed + turn * (used - fixed)) % max(1, count - fixed)
        return jnp.zeros((count,), jnp.int32).at[sequence[jnp.where(places < fixed, places, shifted)]].set(jnp.asarray(lengths, jnp.int32))

    lengths = jnp.where(number % 4 == 0, named(packed, number // 4), named(common, number - number // 4 - 1))
    mixed = jax.random.permutation(jax.random.fold_in(own, 3), count)
    giver, receiver = mixed[0:count // 2 * 2:2], mixed[1:count // 2 * 2:2]
    room = jnp.minimum(lengths[giver] - 1, most - lengths[receiver]) // 2
    room = jnp.where((giver == sequence[0]) | (receiver == sequence[0]) | (lengths[receiver] == 0), 0, jnp.maximum(room, 0))
    shifted = jax.random.randint(jax.random.fold_in(own, 4), (count // 2,), 0, 1 << 20) % (room + 1)
    lengths = lengths.at[giver].add(-shifted).at[receiver].add(shifted)
    items = jnp.searchsorted(jnp.cumsum(lengths), jnp.arange(rows * top), side="right").astype(jnp.int32)
    table = items.reshape(top, rows).T
    table = table[jax.random.permutation(jax.random.fold_in(own, 1), rows)]
    turn = jax.random.randint(jax.random.fold_in(own, 2), (rows, 1), 0, top)
    return jnp.take_along_axis(table, (jnp.arange(top)[None, :] + turn) % top, axis=1)


def portions_of(amount, total, reach, skew, full):
    weights = [(1 << 20) // math.isqrt(standing ** skew) + 1 for standing in range(1, amount + 1)]
    largest = reach if full else min(reach, max(-(-total // amount), total * weights[0] // sum(weights)))
    least = 1 if total - largest >= amount - 1 else 0
    holding, spare = [largest] + [least] * (amount - 1), total - largest - least * (amount - 1)
    while spare > 0:
        free = [i for i in range(1, amount) if holding[i] < largest] or [i for i in range(1, amount) if holding[i] < reach]
        mass, remaining = sum([weights[i] for i in free]), spare
        for i in free:
            addition = min(reach - holding[i], max(1, remaining * weights[i] // mass), spare)
            holding[i] = holding[i] + addition
            spare = spare - addition
    return np.array(holding)


def centred(rng, shape, spread, most, cuts=(), kind=jnp.bfloat16):
    values = spread * jax.random.normal(rng, shape, jnp.float32)
    if cuts:
        values = values * block_levels(rng, shape, cuts, -0.22, 0.18)
    return jnp.clip(values, -most, most).astype(kind)


def setup_inputs(seed: int = 0) -> dict:
    keys = jax.random.split(jax.random.key(seed), 11)
    queries = draw_queries(jax.random.fold_in(keys[10], 71), 0)
    dec_state = centred(keys[1], (UTT, TOKENS, D), 1.0, 6.0, ((0, 16), (1, 16)))
    enc_kv = draw_enc_kv(jax.random.fold_in(keys[10], 71), 0)
    band_start = draw_band_start(jax.random.fold_in(keys[10], 71), 0)
    norm_gain = jnp.clip(1.0 + 0.1 * jax.random.normal(keys[4], (D,), jnp.float32), 0.5, 1.5)
    route_ids_keys = jax.random.split(jax.random.fold_in(keys[5], 1), UTT * TOKENS // TOK_DEV)
    route_ids_turns = jax.random.permutation(jax.random.fold_in(keys[5], 3), UTT * TOKENS // TOK_DEV)
    route_ids = jax.vmap(lambda own, number: deal_out(jax.random.fold_in(keys[5], 2), own, number, TOK_DEV, EXPERTS, 1, CAP, 2))(route_ids_keys, route_ids_turns).reshape((UTT, TOKENS, 1))
    keep = set_ends((jax.random.randint(keys[6], (UTT, TOKENS), 0, 8) < 7).astype(jnp.int32), jax.random.fold_in(keys[6], 1), 0, 1)
    route_prob = jnp.clip(0.25 + 0.75 * jax.random.uniform(keys[7], (UTT, TOKENS), jnp.float32) ** block_levels(keys[7], (UTT, TOKENS), ((0, 16), (1, 16)), -0.2, 0.2), 0.25, 1.0)
    w_in = centred(keys[8], (EXPERTS, FF, D), D ** -0.5, 0.09375, ((0, 16), (1, 16)))
    w_out = centred(keys[9], (EXPERTS, FF, D), FF ** -0.5, 0.078125, ((0, 16), (1, 16)))
    return dict(queries=queries, dec_state=dec_state, enc_kv=enc_kv, band_start=band_start, norm_gain=norm_gain, route_ids=route_ids, keep=keep, route_prob=route_prob, w_in=w_in, w_out=w_out)


def cross_attend(query_rows, band_pair):
    tok_count = query_rows.shape[0]
    groups = HEADS // KV_HEADS
    queries_f = query_rows.astype(jnp.float32).reshape(tok_count, KV_HEADS, groups, DH)
    keys_f = band_pair[0].astype(jnp.float32).reshape(WIN, KV_HEADS, DH)
    values_f = band_pair[1].astype(jnp.float32).reshape(WIN, KV_HEADS, DH)
    scores = jnp.einsum('tkgd,wkd->kgtw', queries_f, keys_f) / math.sqrt(DH)
    row_peak = lax.optimization_barrier(jnp.max(scores, axis=-1, keepdims=True))
    weights = jnp.exp(scores - row_peak)
    row_total = lax.optimization_barrier(jnp.sum(weights, axis=-1))
    rounded = lax.optimization_barrier(weights.astype(jnp.bfloat16)).astype(jnp.float32)
    context = jnp.einsum('kgtw,wkd->tkgd', rounded, values_f) / jnp.transpose(row_total, (2, 0, 1))[..., None]
    return context.reshape(tok_count, HEADS * DH)

def reference(queries, dec_state, enc_kv, band_start, norm_gain, route_ids, keep, route_prob, w_in, w_out):
    producer = jnp.moveaxis(jnp.roll(enc_kv, UTT_SECTION, axis=1), 1, 0)
    query_blocks = queries.reshape(UTT, N_SEQ, TOK_DEV, D)

    def one_block(query_rows, pair, first_frame):
        band_pair = lax.dynamic_slice_in_dim(pair, first_frame.astype(jnp.int32), WIN, 1)
        return cross_attend(query_rows, band_pair)

    def one_utterance(block_rows, pair, firsts):
        return jax.vmap(lambda rows_q, first_frame: one_block(rows_q, pair, first_frame))(block_rows, firsts)
    context = jax.vmap(one_utterance)(query_blocks, producer, band_start).reshape(UTT, TOKENS, D)
    state = dec_state.astype(jnp.float32) + context
    normed = (state * lax.rsqrt(lax.optimization_barrier(jnp.mean(state * state, axis=-1, keepdims=True)) + 1e-06) * norm_gain).astype(jnp.bfloat16)
    flat_rows = normed.reshape(-1, D)
    count_all = flat_rows.shape[0]
    experts_of = route_ids.reshape(-1).astype(jnp.int32)
    row_limit = UTT * N_SEQ * CAP
    order = jnp.argsort(experts_of, stable=True)
    sorted_rows = jnp.concatenate([flat_rows[order], jnp.zeros((row_limit, D), jnp.bfloat16)], axis=0)
    loads = lax.optimization_barrier(jnp.sum((experts_of[None, :] == jnp.arange(EXPERTS, dtype=jnp.int32)[:, None]).astype(jnp.int32), axis=1))
    firsts = (jnp.cumsum(loads) - loads).astype(jnp.int32)

    def per_expert(index, accum):
        begin = firsts[index].astype(jnp.int32)
        chosen = lax.dynamic_slice_in_dim(sorted_rows, begin, row_limit, 0)
        valid = jnp.arange(row_limit, dtype=jnp.int32) < loads[index]
        weight_in = w_in[index]
        hidden = jnp.maximum(jnp.dot(chosen, weight_in.T, preferred_element_type=jnp.float32), 0.0).astype(jnp.bfloat16)
        hidden_f = lax.optimization_barrier(hidden).astype(jnp.float32).reshape(row_limit, GROUP, FS)
        weight_out = w_out[index].astype(jnp.float32).reshape(GROUP, FS, D)
        pieces = jnp.einsum('rgf,gfd->rgd', hidden_f, weight_out)
        pieces = lax.optimization_barrier(pieces.astype(jnp.bfloat16)).astype(jnp.float32)
        summed = lax.optimization_barrier(jnp.sum(pieces, axis=1)).astype(jnp.bfloat16)
        summed = lax.optimization_barrier(summed).astype(jnp.float32)
        result = jnp.where(valid[:, None], summed, jnp.float32(0.0))
        current = lax.dynamic_slice_in_dim(accum, begin, row_limit, 0)
        return lax.dynamic_update_slice_in_dim(accum, current + result, begin, 0)
    accum = lax.fori_loop(0, EXPERTS, per_expert, jnp.zeros((count_all + row_limit, D), jnp.float32))
    expert_out = jnp.zeros((count_all, D), jnp.float32).at[order].set(accum[:count_all])
    scale = (keep.astype(jnp.float32) * route_prob).reshape(-1, 1)
    mixed = (state.reshape(-1, D) + scale * expert_out).astype(jnp.bfloat16)
    return mixed.reshape(UTT, TOKENS, D)
```

```python
import math

import jax
import jax.numpy as jnp
import numpy as np
from jax import lax
from jax.experimental import pallas as pl
from jax.experimental.pallas import tpu as pltpu
from jax.sharding import PartitionSpec as P

D = 4096
HEADS = 32
KV_HEADS = 8
DH = 128
WIN = 128
MESH = pl.DeviceIdType.MESH

TOK = 96
HALF = 48
SEGS = 8
SEG = D // SEGS
MSG = 24
PEERS = 16
FS = 320
PA = (0, 1152)
PB = (1152, 1152)
QA = (2304, 896)
QB = (3200, 896)
PP = (0, 2304)
QQ = (2304, 1792)


def shifted(block, axis, distance):
    devices = range(lax.axis_size(axis))
    route = [((i - distance) % len(devices), i) for i in devices]
    return lax.ppermute(block, axis, route)


def extended(cells, sides, width):
    for axis, dim in sides:
        count = lax.axis_size(axis)
        ends = count - 1
        head = lax.slice_in_dim(cells, 0, width, axis=dim)
        tail = lax.slice_in_dim(cells, cells.shape[dim] - width, cells.shape[dim], axis=dim)
        cells = jnp.concatenate(
            [
                lax.ppermute(tail, axis, [(i, (i + 1) % count) for i in range(ends)]),
                cells,
                lax.ppermute(head, axis, [((i + 1) % count, i) for i in range(ends)]),
            ],
            axis=dim,
        )
    return cells


def cross_attend(query_rows, band_pair):
    tok_count = query_rows.shape[0]
    groups = HEADS // KV_HEADS
    grouped = query_rows.reshape(tok_count, KV_HEADS, groups, DH)
    keys_b = band_pair[0].reshape(WIN, KV_HEADS, DH)
    values_b = band_pair[1].reshape(WIN, KV_HEADS, DH)
    scores = jnp.einsum(
        "tkgd,wkd->kgtw", grouped, keys_b, preferred_element_type=jnp.float32
    ) / math.sqrt(DH)
    row_peak = jnp.max(scores, axis=-1, keepdims=True)
    weights = jnp.exp(scores - row_peak)
    row_total = jnp.sum(weights, axis=-1)
    rounded = weights.astype(jnp.bfloat16)
    context = jnp.einsum("kgtw,wkd->tkgd", rounded, values_b, preferred_element_type=jnp.float32)
    context = context / jnp.transpose(row_total, (2, 0, 1))[..., None]
    return context.reshape(tok_count, HEADS * DH)


def message_order():
    order = np.zeros((SEGS * HALF, SEGS * HALF), np.float32)
    for seg in range(SEGS):
        for peer in range(PEERS):
            for j in range(3):
                order[seg * HALF + peer * 3 + j, peer * MSG + seg * 3 + j] = 1.0
    return order


def moe_kernel(
    unpack_ref, pack_ref, normed_ref, state_ref, ids_col_ref, ids_row_ref, scale_ref, w_in_hbm, w_out_hbm,
    out_ref,
    win, wout, hid, xg, pt, out_msg, in_msg, ret_msg, ret_in, fin,
    r_p2r, r_p2l, r_pr, r_pl, r_py, r_qy, r_q2r, r_q2l, r_qr, r_ql,
    w_sem, wx_ssem, wx_rsem, a_ssem, a_rsem, b_ssem, b_rsem, self_sem, g_ssem, g_rsem, s_ssem, s_rsem,
):
    s = lax.axis_index("section")
    q = lax.axis_index("seq")
    x = lax.axis_index("expert")
    l, c = s // 2, s % 2
    yh, z = q // 8, q % 8
    me = z * 2 + c

    def dev(x_, l_, c_, yh_, z_):
        return (l_ * 2 + c_, yh_ * 8 + z_, x_)

    xr, xl, xo = (x + 1) % 4, (x + 3) % 4, (x + 2) % 4
    right, left = dev(xr, l, c, yh, z), dev(xl, l, c, yh, z)
    across, sibling = dev(x, 1 - l, c, yh, z), dev(x, l, 1 - c, yh, z)

    def peer(wave, d):
        if wave == 0:
            return dev(x, l, d % 2, yh, d // 2)
        return dev(x, 1 - l, d % 2, 1 - yh, d // 2)

    w_local = [
        pltpu.make_async_copy(w_in_hbm.at[c], win.at[pl.ds(0, FS)], w_sem.at[0]),
        pltpu.make_async_copy(w_out_hbm.at[c], wout.at[pl.ds(0, FS)], w_sem.at[1]),
    ]
    for cp in w_local:
        cp.start()

    barrier = pltpu.get_barrier_semaphore()
    for there in (right, left, across):
        pl.semaphore_signal(barrier, inc=1, device_id=there, device_id_type=MESH)

    @pl.loop(1, PEERS)
    def _(i):
        pl.semaphore_signal(barrier, inc=1, device_id=peer(0, (me + i) % PEERS), device_id_type=MESH)

    @pl.loop(0, PEERS)
    def _(i):
        pl.semaphore_signal(barrier, inc=1, device_id=peer(1, (me + i) % PEERS), device_id_type=MESH)

    ids_c, ids_r = ids_col_ref[...], ids_row_ref[...]
    sub = lax.broadcasted_iota(jnp.int32, (TOK, TOK), 0)
    lane = lax.broadcasted_iota(jnp.int32, (TOK, TOK), 1)
    same = ids_c == ids_r
    rank_c = jnp.sum(jnp.where(same & (lane < sub), 1.0, 0.0), axis=1, keepdims=True)
    rank_r = jnp.sum(jnp.where(same & (sub < lane), 1.0, 0.0), axis=0, keepdims=True)

    def slot(ids, rank):
        hi = jnp.where(ids >= PEERS, 1, 0)
        wave = hi + yh - 2 * hi * yh
        return ((wave * PEERS + ids - hi * PEERS) * 3).astype(jnp.float32) + rank

    perm = (slot(ids_r, rank_r) == sub.astype(jnp.float32)).astype(jnp.bfloat16)
    perm_t = (slot(ids_c, rank_c) == lane.astype(jnp.float32)).astype(jnp.bfloat16)

    def dot(a, b):
        return jnp.dot(a, b, preferred_element_type=jnp.float32)

    def pack(rows):
        return dot(pack_ref[...], jnp.concatenate([rows[:, g * SEG : (g + 1) * SEG] for g in range(SEGS)], axis=0)).astype(jnp.bfloat16)

    def a_copy(wave, d):
        return pltpu.make_async_remote_copy(
            src_ref=out_msg.at[wave, d], dst_ref=in_msg.at[wave, me],
            send_sem=a_ssem.at[wave, d], recv_sem=a_rsem.at[wave, me],
            device_id=peer(wave, d), device_id_type=MESH,
        )

    def a_recv(wave, d):
        return pltpu.make_async_remote_copy(
            src_ref=out_msg.at[wave, d], dst_ref=in_msg.at[wave, d],
            send_sem=a_ssem.at[wave, d], recv_sem=a_rsem.at[wave, d],
            device_id=peer(wave, d), device_id_type=MESH,
        )

    def b_copy(wave, d):
        return pltpu.make_async_remote_copy(
            src_ref=ret_msg.at[wave, d], dst_ref=ret_in.at[wave, me],
            send_sem=b_ssem.at[wave, d], recv_sem=b_rsem.at[wave, me],
            device_id=peer(wave, d), device_id_type=MESH,
        )

    def b_recv(wave, d):
        return pltpu.make_async_remote_copy(
            src_ref=ret_msg.at[wave, d], dst_ref=ret_in.at[wave, d],
            send_sem=b_ssem.at[wave, d], recv_sem=b_rsem.at[wave, d],
            device_id=peer(wave, d), device_id_type=MESH,
        )

    def each_peer(wave, act):
        @pl.loop(1 if wave == 0 else 0, PEERS)
        def _(i):
            act((me + i) % PEERS)

    self_a = pltpu.make_async_copy(out_msg.at[0, me], in_msg.at[0, me], self_sem.at[0])
    self_b = pltpu.make_async_copy(ret_msg.at[0, me], ret_in.at[0, me], self_sem.at[1])

    def outgoing(wave):
        rows = dot(perm[wave * HALF : (wave + 1) * HALF], normed_ref[...]).astype(jnp.bfloat16)
        out_msg[wave] = pack(rows).reshape(PEERS, MSG, SEG)

    outgoing(0)
    pl.semaphore_wait(barrier, 34)
    each_peer(0, lambda d: a_copy(0, d).start())
    self_a.start()
    outgoing(1)
    each_peer(1, lambda d: a_copy(1, d).start())

    w_swap = [
        pltpu.make_async_remote_copy(
            src_ref=hbm.at[1 - c], dst_ref=vmem.at[pl.ds(FS, FS)], send_sem=wx_ssem.at[i], recv_sem=wx_rsem.at[i],
            device_id=sibling, device_id_type=MESH,
        )
        for i, (hbm, vmem) in enumerate(((w_in_hbm, win), (w_out_hbm, wout)))
    ]
    for cp in w_swap:
        cp.start()

    own, mate = x * 2 + l, x * 2 + 1 - l

    def blk(x_, far=False):
        return x_ * 2 + (1 - l if far else l)

    gather = [
        (own, PP, across, mate),
        (own, QQ, right, blk(xl)),
        (own, QQ, left, blk(xr)),
        (own, PP, right, blk(xl)),
        (own, PP, left, blk(xr)),
        (own, QQ, across, mate),
        (mate, PP, right, blk(xl, True)),
        (mate, PP, left, blk(xr, True)),
        (blk(xl), QA, right, blk(xo)),
        (blk(xr), QB, left, blk(xo)),
        (blk(xl), QQ, across, blk(xl, True)),
        (blk(xr), QQ, across, blk(xr, True)),
        (blk(xl), PA, right, blk(xo)),
        (blk(xr), PB, left, blk(xo)),
        (blk(xl, True), PA, right, blk(xo, True)),
        (blk(xr, True), PB, left, blk(xo, True)),
        (blk(xo), QA, across, blk(xo, True)),
        (blk(xo), QB, across, blk(xo, True)),
    ]

    def g_copy(wave, i, received=False):
        sent, cols, there, got = gather[i]
        ref = xg.at[wave, got if received else sent, :, pl.ds(*cols)]
        return pltpu.make_async_remote_copy(
            src_ref=ref, dst_ref=ref, send_sem=g_ssem.at[wave, i], recv_sem=g_rsem.at[wave, i],
            device_id=there, device_id_type=MESH,
        )

    def g_start(wave, *which):
        for i in which:
            g_copy(wave, i).start()

    def g_wait(wave, *which):
        for i in which:
            g_copy(wave, i, True).wait_recv()

    def arrive(wave):
        if wave == 0:
            self_a.wait()
        each_peer(wave, lambda d: a_recv(wave, d).wait_recv())
        rows = dot(unpack_ref[...], in_msg[wave].reshape(PEERS * MSG, SEG)).astype(jnp.bfloat16)
        for g in range(SEGS):
            xg[wave, own, :, pl.ds(g * SEG, SEG)] = rows[g * HALF : (g + 1) * HALF]

    def gather_1(wave):
        g_start(wave, 0, 1, 2, 3, 4, 5)

    def gather_2(wave):
        g_wait(wave, 0)
        g_start(wave, 6, 7)
        g_wait(wave, 1, 2)
        g_start(wave, 8, 9, 10, 11)

    def gather_3(wave):
        g_wait(wave, 3, 4)
        g_start(wave, 12, 13)
        g_wait(wave, 6, 7)
        g_start(wave, 14, 15)
        g_wait(wave, 8, 9)
        g_start(wave, 16, 17)

    def gather_4(wave):
        g_wait(wave, 5, 10, 11, 12, 13, 14, 15, 16, 17)

    def hidden(wave):
        rows = xg[wave].reshape(8 * HALF, D)
        units = lax.dot_general(rows, win[...], (((1,), (1,)), ((), ())), preferred_element_type=jnp.float32)
        hid[...] = jnp.maximum(units, 0.0).astype(jnp.bfloat16)

    def partial(wave, cols):
        part = dot(hid[...], wout[:, pl.ds(*cols)])
        pt[wave, :, :, pl.ds(*cols)] = part.astype(jnp.bfloat16).reshape(8, HALF, cols[1])

    def span(home, cols):
        return lambda wave: pt.at[wave, home, :, pl.ds(*cols)]

    def inner(buf, i, cols):
        return lambda wave: buf.at[wave, i, :, pl.ds(*cols)]

    sums = []
    for f in (1, 0):
        far = f == 1
        sums += [
            (span(blk(xo, far), PA), inner(r_p2r, f, PA), left),
            (span(blk(xo, far), PB), inner(r_p2l, f, PA), right),
            (span(blk(xl, far), PB), inner(r_pr, f, PB), left),
            (span(blk(xr, far), PA), inner(r_pl, f, PA), right),
            (span(blk(xl, far), PA), inner(r_pr, f, PA), left),
            (span(blk(xr, far), PB), inner(r_pl, f, PB), right),
        ]
    q0, q1 = (0, QA[1]), (QA[1], QB[1])
    sums += [
        (span(mate, PP), inner(r_py, 0, PP), across),
        (span(blk(xo, True), QQ), inner(r_qy, 0, (0, QQ[1])), across),
        (span(blk(xl, True), QQ), inner(r_qy, 1, (0, QQ[1])), across),
        (span(blk(xr, True), QQ), inner(r_qy, 2, (0, QQ[1])), across),
        (span(mate, QQ), inner(r_qy, 3, (0, QQ[1])), across),
        (span(blk(xo), QA), inner(r_q2r, 0, q0), left),
        (span(blk(xo), QB), inner(r_q2l, 0, q0), right),
        (span(blk(xl), QB), inner(r_qr, 0, q1), left),
        (span(blk(xr), QA), inner(r_ql, 0, q0), right),
        (span(blk(xl), QA), inner(r_qr, 0, q0), left),
        (span(blk(xr), QB), inner(r_ql, 0, q1), right),
    ]

    def s_copy(wave, i):
        src, dst, there = sums[i]
        return pltpu.make_async_remote_copy(
            src_ref=src(wave), dst_ref=dst(wave), send_sem=s_ssem.at[wave, i], recv_sem=s_rsem.at[wave, i],
            device_id=there, device_id_type=MESH,
        )

    def s_start(wave, *which):
        for i in which:
            s_copy(wave, i).start()

    def s_wait(wave, *which):
        for i in which:
            s_copy(wave, i).wait_recv()

    def add(wave, home, cols, *terms):
        step = 128

        @pl.loop(0, cols[1] // step)
        def _(i):
            here = pl.ds(pl.multiple_of(cols[0] + i * step, 128), step)
            total = pt[wave, home, :, here].astype(jnp.float32)
            for buf, j, first in terms:
                total += buf[wave, j, :, pl.ds(pl.multiple_of(first + i * step, 128), step)].astype(jnp.float32)
            pt[wave, home, :, here] = total.astype(jnp.bfloat16)

    def sum_p2(wave):
        for n, f in ((0, 1), (6, 0)):
            far = f == 1
            s_wait(wave, n, n + 1)
            add(wave, blk(xl, far), PA, (r_p2r, f, 0))
            s_start(wave, n + 4)
            add(wave, blk(xr, far), PB, (r_p2l, f, 0))
            s_start(wave, n + 5)

    def sum_p1(wave):
        for n, f in ((0, 1), (6, 0)):
            s_wait(wave, n + 2, n + 3, n + 4, n + 5)
            add(wave, blk(x, f == 1), PP, (r_pr, f, 0), (r_pl, f, 0))
            if f == 1:
                s_start(wave, 12)

    def sum_py(wave):
        s_wait(wave, 12)
        add(wave, own, PP, (r_py, 0, 0))

    def sum_qy(wave):
        s_wait(wave, 13)
        add(wave, blk(xo), QQ, (r_qy, 0, 0))
        s_start(wave, 17, 18)
        s_wait(wave, 14)
        add(wave, blk(xl), QQ, (r_qy, 1, 0))
        s_start(wave, 19)
        s_wait(wave, 15)
        add(wave, blk(xr), QQ, (r_qy, 2, 0))
        s_start(wave, 20)

    def sum_q2(wave):
        s_wait(wave, 17, 18)
        add(wave, blk(xl), QA, (r_q2r, 0, 0))
        s_start(wave, 21)
        add(wave, blk(xr), QB, (r_q2l, 0, 0))
        s_start(wave, 22)

    def sum_q1(wave):
        s_wait(wave, 16, 19, 20, 21, 22)
        add(wave, own, QQ, (r_qy, 3, 0), (r_qr, 0, 0), (r_ql, 0, 0))

    def send_back(wave):
        ret_msg[wave] = pack(pt[wave, own]).reshape(PEERS, MSG, SEG)
        each_peer(wave, lambda d: b_copy(wave, d).start())
        if wave == 0:
            self_b.start()

    def come_back(wave):
        if wave == 0:
            self_b.wait()
        each_peer(wave, lambda d: b_recv(wave, d).wait_recv())
        fin[wave] = dot(unpack_ref[...], ret_in[wave].reshape(PEERS * MSG, SEG)).astype(jnp.bfloat16)

    def partials(wave):
        partial(wave, PA)
        s_start(wave, 0, 6, 3, 9)
        partial(wave, QA)
        partial(wave, QB)
        s_start(wave, 13, 14, 15, 16)
        partial(wave, PB)
        s_start(wave, 1, 7, 2, 8)

    arrive(0)
    gather_1(0)
    gather_2(0)
    arrive(1)
    gather_3(0)
    gather_1(1)
    gather_4(0)
    for cp in w_local:
        cp.wait()
    for cp in w_swap:
        cp.wait_recv()
    hidden(0)
    gather_2(1)
    partials(0)
    gather_3(1)
    sum_qy(0)
    sum_p2(0)
    gather_4(1)
    hidden(1)
    sum_q2(0)
    sum_p1(0)
    partials(1)
    sum_q1(0)
    sum_py(0)
    send_back(0)
    sum_qy(1)
    sum_p2(1)
    sum_q2(1)
    sum_p1(1)
    sum_q1(1)
    sum_py(1)
    send_back(1)
    come_back(0)
    come_back(1)

    for g in range(SEGS):
        cols = pl.ds(g * SEG, SEG)
        rows = jnp.concatenate([fin[0, pl.ds(g * HALF, HALF)], fin[1, pl.ds(g * HALF, HALF)]], axis=0)
        expert_out = dot(perm_t, rows)
        out_ref[:, cols] = (state_ref[:, cols] + scale_ref[...] * expert_out).astype(jnp.bfloat16)

    for cp in w_swap:
        cp.wait_send()
    for wave in (0, 1):
        each_peer(wave, lambda d: a_recv(wave, d).wait_send())
        each_peer(wave, lambda d: b_recv(wave, d).wait_send())
        for i in range(len(gather)):
            g_copy(wave, i).wait_send()
        for i in range(len(sums)):
            s_copy(wave, i).wait_send()


def expert_layer(normed, state, ids, scale, w_in, w_out):
    order = message_order()
    vmem = pl.BlockSpec(memory_space=pltpu.VMEM)
    hbm = pl.BlockSpec(memory_space=pl.ANY)
    bf = jnp.bfloat16
    return pl.pallas_call(
        moe_kernel,
        out_shape=jax.ShapeDtypeStruct((TOK, D), bf),
        in_specs=[vmem] * 7 + [hbm] * 2,
        out_specs=vmem,
        scratch_shapes=[
            pltpu.VMEM((2 * FS, D), bf),
            pltpu.VMEM((2 * FS, D), bf),
            pltpu.VMEM((8 * HALF, 2 * FS), bf),
            pltpu.VMEM((2, 8, HALF, D), bf),
            pltpu.VMEM((2, 8, HALF, D), bf),
            pltpu.VMEM((2, PEERS, MSG, SEG), bf),
            pltpu.VMEM((2, PEERS, MSG, SEG), bf),
            pltpu.VMEM((2, PEERS, MSG, SEG), bf),
            pltpu.VMEM((2, PEERS, MSG, SEG), bf),
            pltpu.VMEM((2, PEERS * MSG, SEG), bf),
            pltpu.VMEM((2, 2, HALF, PA[1]), bf),
            pltpu.VMEM((2, 2, HALF, PB[1]), bf),
            pltpu.VMEM((2, 2, HALF, PP[1]), bf),
            pltpu.VMEM((2, 2, HALF, PP[1]), bf),
            pltpu.VMEM((2, 1, HALF, PP[1]), bf),
            pltpu.VMEM((2, 4, HALF, QQ[1]), bf),
            pltpu.VMEM((2, 1, HALF, QA[1]), bf),
            pltpu.VMEM((2, 1, HALF, QB[1]), bf),
            pltpu.VMEM((2, 1, HALF, QQ[1]), bf),
            pltpu.VMEM((2, 1, HALF, QQ[1]), bf),
            pltpu.SemaphoreType.DMA((2,)),
            pltpu.SemaphoreType.DMA((2,)),
            pltpu.SemaphoreType.DMA((2,)),
            pltpu.SemaphoreType.DMA((2, PEERS)),
            pltpu.SemaphoreType.DMA((2, PEERS)),
            pltpu.SemaphoreType.DMA((2, PEERS)),
            pltpu.SemaphoreType.DMA((2, PEERS)),
            pltpu.SemaphoreType.DMA((2,)),
            pltpu.SemaphoreType.DMA((2, 18)),
            pltpu.SemaphoreType.DMA((2, 18)),
            pltpu.SemaphoreType.DMA((2, 23)),
            pltpu.SemaphoreType.DMA((2, 23)),
        ],
        compiler_params=pltpu.CompilerParams(
            collective_id=0, has_side_effects=True, vmem_limit_bytes=60 * 2**20
        ),
    )(
        jnp.asarray(order, bf),
        jnp.asarray(order.T, bf),
        normed,
        state,
        ids.reshape(TOK, 1),
        ids.reshape(1, TOK),
        scale.reshape(TOK, 1),
        w_in,
        w_out,
    )


def body(
    queries, dec_state, enc_kv, band_start, norm_gain, route_ids, keep, route_prob, w_in, w_out
):
    own_pair = shifted(enc_kv[:, 0], "section", 1)
    frames_dev = own_pair.shape[1]
    offset = band_start[0, 0]
    position = lax.axis_index("seq")
    widened = extended(own_pair, (("seq", 1),), frames_dev)
    local_first = offset - (position - 1) * frames_dev
    band_pair = lax.dynamic_slice_in_dim(widened, local_first, WIN, 1)
    context = cross_attend(queries[0], band_pair)
    state = dec_state[0].astype(jnp.float32) + context
    normed = (
        state * lax.rsqrt(jnp.mean(state * state, axis=-1, keepdims=True) + 1e-06) * norm_gain
    ).astype(jnp.bfloat16)
    scale = keep[0].astype(jnp.float32) * route_prob[0]
    return expert_layer(normed, state, route_ids[0], scale, w_in, w_out)[None]


def solution(mesh):
    return jax.shard_map(
        body,
        mesh=mesh,
        in_specs=(
            P(("section", "expert"), "seq", None),
            P(("section", "expert"), "seq", None),
            P(None, ("section", "expert"), "seq", None),
            P(("section", "expert"), "seq"),
            P(),
            P(("section", "expert"), "seq", None),
            P(("section", "expert"), "seq"),
            P(("section", "expert"), "seq"),
            P("seq", ("section", "expert"), None),
            P("seq", ("section", "expert"), None),
        ),
        out_specs=P(("section", "expert"), "seq", None),
        check_vma=False,
    )
```

```python
import math

import jax
import jax.numpy as jnp
import numpy as np
from jax import lax
from jax.experimental import pallas as pl
from jax.experimental.pallas import tpu as pltpu
from jax.sharding import PartitionSpec as P

D = 4096
HEADS = 32
KV_HEADS = 8
DH = 128
WIN = 128
MESH = pl.DeviceIdType.MESH

TOK = 96
HALF = 48
SEGS = 8
SEG = D // SEGS
MSG = 24
PEERS = 16
FS = 320
PA = (0, 1152)
PB = (1152, 1152)
QA = (2304, 896)
QB = (3200, 896)
PP = (0, 2304)
QQ = (2304, 1792)
FR = 160
KVC = 512
GROUP = HEADS // KV_HEADS


def message_order():
    order = np.zeros((SEGS * HALF, SEGS * HALF), np.float32)
    for seg in range(SEGS):
        for peer in range(PEERS):
            for j in range(3):
                order[seg * HALF + peer * 3 + j, peer * MSG + seg * 3 + j] = 1.0
    return order


def moe_kernel(
    first_ref, ids_ref, keep_ref, prob_ref, gain_ref,
    unpack_hbm, pack_hbm, queries_hbm, dec_hbm, kv_hbm, w_in_hbm, w_out_hbm,
    out_ref,
    unpack_ref, pack_ref, queries_ref, dec_ref, state_ref, normed_ref, kv,
    in_sem, k_ssem, k_rsem, f_ssem, f_rsem, x_ssem,
    win, wout, hid, xg, pt, out_msg, in_msg, ret_msg, ret_in, fin,
    r_p2r, r_p2l, r_pr, r_pl, r_py, r_qy, r_q2r, r_q2l, r_qr, r_ql,
    w_sem, wx_ssem, wx_rsem, a_ssem, a_rsem, b_ssem, b_rsem, self_sem, g_ssem, g_rsem, s_ssem, s_rsem,
):
    s = lax.axis_index("section")
    q = lax.axis_index("seq")
    x = lax.axis_index("expert")
    l, c = s // 2, s % 2
    yh, z = q // 8, q % 8
    me = z * 2 + c

    def dev(x_, l_, c_, yh_, z_):
        return (l_ * 2 + c_, yh_ * 8 + z_, x_)

    xr, xl, xo = (x + 1) % 4, (x + 3) % 4, (x + 2) % 4
    right, left = dev(xr, l, c, yh, z), dev(xl, l, c, yh, z)
    across, sibling = dev(x, 1 - l, c, yh, z), dev(x, l, 1 - c, yh, z)

    def peer(wave, d):
        if wave == 0:
            return dev(x, l, d % 2, yh, d // 2)
        return dev(x, 1 - l, d % 2, 1 - yh, d // 2)

    w_local = [
        pltpu.make_async_copy(w_in_hbm.at[c], win.at[pl.ds(0, FS)], w_sem.at[0]),
        pltpu.make_async_copy(w_out_hbm.at[c], wout.at[pl.ds(0, FS)], w_sem.at[1]),
    ]
    inputs = [
        pltpu.make_async_copy(src, dst, in_sem.at[i])
        for i, (src, dst) in enumerate(
            (
                (queries_hbm.at[0], queries_ref),
                (dec_hbm.at[0], dec_ref),
                (pack_hbm, pack_ref),
                (unpack_hbm, unpack_ref),
            )
        )
    ]

    barrier = pltpu.get_barrier_semaphore()
    corner = dev(x, 1 - l, 1 - c, yh, z)
    after, before = ((s, (q + 1) % 16, x), (s, (q + 15) % 16, x))
    opposite = dev(x, l, c, 1 - yh, z)
    for there in (corner, opposite, after, before, right, left, across):
        pl.semaphore_signal(barrier, inc=1, device_id=there, device_id_type=MESH)

    @pl.loop(1, PEERS)
    def _(i):
        pl.semaphore_signal(barrier, inc=1, device_id=peer(0, (me + i) % PEERS), device_id_type=MESH)

    @pl.loop(0, PEERS)
    def _(i):
        pl.semaphore_signal(barrier, inc=1, device_id=peer(1, (me + i) % PEERS), device_id_type=MESH)

    for cp in inputs:
        cp.start()
    for cp in w_local:
        cp.start()

    sub = lax.broadcasted_iota(jnp.int32, (TOK, TOK), 0)
    lane = lax.broadcasted_iota(jnp.int32, (TOK, TOK), 1)

    def column(row):
        return jnp.sum(jnp.where(sub == lane, row, 0.0), axis=1, keepdims=True)

    ids_r = ids_ref[...].astype(jnp.float32)
    ids_c = column(ids_r)
    scale = column(keep_ref[...].astype(jnp.float32) * prob_ref[...])
    same = ids_c == ids_r
    rank_c = jnp.sum(jnp.where(same & (lane < sub), 1.0, 0.0), axis=1, keepdims=True)
    rank_r = jnp.sum(jnp.where(same & (sub < lane), 1.0, 0.0), axis=0, keepdims=True)

    def slot(ids, rank):
        hi = jnp.where(ids >= PEERS, 1.0, 0.0)
        here = yh.astype(jnp.float32)
        wave = hi + here - 2.0 * hi * here
        return (wave * PEERS + ids - hi * PEERS) * 3.0 + rank

    perm = (slot(ids_r, rank_r) == sub.astype(jnp.float32)).astype(jnp.bfloat16)
    perm_t = (slot(ids_c, rank_c) == lane.astype(jnp.float32)).astype(jnp.bfloat16)

    def dot(a, b):
        return jnp.dot(a, b, preferred_element_type=jnp.float32)

    def pack(rows):
        return dot(pack_ref[...], jnp.concatenate([rows[:, g * SEG : (g + 1) * SEG] for g in range(SEGS)], axis=0)).astype(jnp.bfloat16)

    def a_copy(wave, d):
        return pltpu.make_async_remote_copy(
            src_ref=out_msg.at[wave, d], dst_ref=in_msg.at[wave, me],
            send_sem=a_ssem.at[wave, d], recv_sem=a_rsem.at[wave, me],
            device_id=peer(wave, d), device_id_type=MESH,
        )

    def a_recv(wave, d):
        return pltpu.make_async_remote_copy(
            src_ref=out_msg.at[wave, d], dst_ref=in_msg.at[wave, d],
            send_sem=a_ssem.at[wave, d], recv_sem=a_rsem.at[wave, d],
            device_id=peer(wave, d), device_id_type=MESH,
        )

    def b_copy(wave, d):
        return pltpu.make_async_remote_copy(
            src_ref=ret_msg.at[wave, d], dst_ref=ret_in.at[wave, me],
            send_sem=b_ssem.at[wave, d], recv_sem=b_rsem.at[wave, me],
            device_id=peer(wave, d), device_id_type=MESH,
        )

    def b_recv(wave, d):
        return pltpu.make_async_remote_copy(
            src_ref=ret_msg.at[wave, d], dst_ref=ret_in.at[wave, d],
            send_sem=b_ssem.at[wave, d], recv_sem=b_rsem.at[wave, d],
            device_id=peer(wave, d), device_id_type=MESH,
        )

    def each_peer(wave, act):
        @pl.loop(1 if wave == 0 else 0, PEERS)
        def _(i):
            act((me + i) % PEERS)

    self_a = pltpu.make_async_copy(out_msg.at[0, me], in_msg.at[0, me], self_sem.at[0])
    self_b = pltpu.make_async_copy(ret_msg.at[0, me], ret_in.at[0, me], self_sem.at[1])

    def outgoing(wave):
        rows = dot(perm[wave * HALF : (wave + 1) * HALF], normed_ref[...]).astype(jnp.bfloat16)
        out_msg[wave] = pack(rows).reshape(PEERS, MSG, SEG)

    nxt = ((s + 1) % 4, q, x)

    def chunk(i):
        return i % 2, pl.ds((i // 2) * KVC, KVC)

    def k_copy(i):
        which, cols = chunk(i)
        return pltpu.make_async_remote_copy(
            src_ref=kv_hbm.at[which, 0, :, cols], dst_ref=kv.at[which, 1, :, cols],
            send_sem=k_ssem.at[i], recv_sem=k_rsem.at[i], device_id=nxt, device_id_type=MESH,
        )

    RELAYED = 2
    ring_after, ring_before = dev(x, l, c, yh, (z + 1) % 8), dev(x, l, c, yh, (z + 7) % 8)

    def f_copy(i, up):
        which, cols = chunk(i)
        to = 0 if up else 2
        if i < RELAYED:
            there = ring_after if up else ring_before
        else:
            there = after if up else before
        return pltpu.make_async_remote_copy(
            src_ref=kv.at[which, 1, :, cols], dst_ref=kv.at[which, to, :, cols],
            send_sem=f_ssem.at[i, to // 2], recv_sem=f_rsem.at[i, to // 2],
            device_id=there, device_id_type=MESH,
        )

    def relay_copy(i, up):
        which, cols = chunk(i)
        to = 0 if up else 2
        return pltpu.make_async_remote_copy(
            src_ref=kv.at[which, to, :, cols], dst_ref=kv.at[which, to, :, cols],
            send_sem=x_ssem.at[i, to // 2], recv_sem=f_rsem.at[i, to // 2],
            device_id=opposite, device_id_type=MESH,
        )

    is_first, is_last = q == 0, q == 15

    def relay(i):
        for edge, up in ((is_first, True), (is_last, False)):

            @pl.when(edge)
            def _():
                f_copy(i, up).wait_recv()
                relay_copy(i, up).start()

    for edge, to in ((is_first, 0), (is_last, 2)):

        @pl.when(edge)
        def _():
            for which in (0, 1):
                kv[which, to, :, pl.ds(KVC, KVC)] = jnp.zeros((FR, KVC), jnp.bfloat16)

    def neighbours(act_up, act_down, up_edge, down_edge):
        pl.when(jnp.logical_not(up_edge))(act_up)
        pl.when(jnp.logical_not(down_edge))(act_down)

    pl.semaphore_wait(barrier, 38)
    for i in range(4):
        k_copy(i).start()
    for i in range(4):
        k_copy(i).wait_recv()
        neighbours(lambda: f_copy(i, True).start(), lambda: f_copy(i, False).start(), is_last, is_first)
        if 1 <= i <= RELAYED:
            relay(i - 1)

    w_swap = [
        pltpu.make_async_remote_copy(
            src_ref=hbm.at[1 - c], dst_ref=vmem.at[pl.ds(FS, FS)], send_sem=wx_ssem.at[i], recv_sem=wx_rsem.at[i],
            device_id=sibling, device_id_type=MESH,
        )
        for i, (hbm, vmem) in enumerate(((w_in_hbm, win), (w_out_hbm, wout)))
    ]
    for cp in w_swap:
        cp.start()

    for cp in inputs:
        cp.wait()
    first = first_ref[0, 0] - (q - 1) * FR
    frame = lax.broadcasted_iota(jnp.int32, (WIN, 3 * FR), 1)
    row = lax.broadcasted_iota(jnp.int32, (WIN, 3 * FR), 0)
    band = jnp.where(frame == row + first, 1.0, 0.0).astype(jnp.bfloat16)
    squares = jnp.zeros((TOK, DH), jnp.float32)
    for part in (0, 1):
        for i in (2 * part, 2 * part + 1):
            neighbours(
                lambda: f_copy(i, True).wait_recv(), lambda: f_copy(i, False).wait_recv(), is_first, is_last
            )
        part_cols = pl.ds(part * KVC, KVC)
        keys, values = (
            dot(band, kv[which, :, :, part_cols].reshape(3 * FR, KVC)).astype(jnp.bfloat16) for which in (0, 1)
        )
        for h in range(KV_HEADS // 2):
            at = slice(h * DH, (h + 1) * DH)
            heads = [pl.ds(((part * 4 + h) * GROUP + g) * DH, DH) for g in range(GROUP)]
            rows = jnp.concatenate([queries_ref[:, cols] for cols in heads], axis=0)
            scores = lax.dot_general(
                rows, keys[:, at], (((1,), (1,)), ((), ())), preferred_element_type=jnp.float32
            ) * (1.0 / math.sqrt(DH))
            weights = jnp.exp(scores - jnp.max(scores, axis=1, keepdims=True))
            total = jnp.sum(weights, axis=1, keepdims=True)
            context = dot(weights.astype(jnp.bfloat16), values[:, at]) / total
            for g, cols in enumerate(heads):
                state = dec_ref[:, cols].astype(jnp.float32) + context[g * TOK : (g + 1) * TOK]
                state_ref[:, cols] = state
                squares += state * state
    inverse = lax.rsqrt(jnp.sum(squares, axis=1, keepdims=True) * (1.0 / D) + 1e-06)
    for h in range(HEADS):
        cols = pl.ds(h * DH, DH)
        normed_ref[:, cols] = (state_ref[:, cols] * inverse * gain_ref[:, cols]).astype(jnp.bfloat16)

    outgoing(0)
    each_peer(0, lambda d: a_copy(0, d).start())
    self_a.start()
    outgoing(1)

    own, mate = x * 2 + l, x * 2 + 1 - l

    def blk(x_, far=False):
        return x_ * 2 + (1 - l if far else l)

    gather = [
        (own, PP, across, mate),
        (own, QQ, right, blk(xl)),
        (own, QQ, left, blk(xr)),
        (own, PP, right, blk(xl)),
        (own, PP, left, blk(xr)),
        (own, QQ, across, mate),
        (mate, PP, right, blk(xl, True)),
        (mate, PP, left, blk(xr, True)),
        (blk(xl), QA, right, blk(xo)),
        (blk(xr), QB, left, blk(xo)),
        (blk(xl), QQ, across, blk(xl, True)),
        (blk(xr), QQ, across, blk(xr, True)),
        (blk(xl), PA, right, blk(xo)),
        (blk(xr), PB, left, blk(xo)),
        (blk(xl, True), PA, right, blk(xo, True)),
        (blk(xr, True), PB, left, blk(xo, True)),
        (blk(xo), QA, across, blk(xo, True)),
        (blk(xo), QB, across, blk(xo, True)),
    ]

    def g_copy(wave, i, received=False):
        sent, cols, there, got = gather[i]
        ref = xg.at[wave, got if received else sent, :, pl.ds(*cols)]
        return pltpu.make_async_remote_copy(
            src_ref=ref, dst_ref=ref, send_sem=g_ssem.at[wave, i], recv_sem=g_rsem.at[wave, i],
            device_id=there, device_id_type=MESH,
        )

    def g_start(wave, *which):
        for i in which:
            g_copy(wave, i).start()

    def g_wait(wave, *which):
        for i in which:
            g_copy(wave, i, True).wait_recv()

    def arrive(wave):
        if wave == 0:
            self_a.wait()
        each_peer(wave, lambda d: a_recv(wave, d).wait_recv())
        if wave == 0:
            each_peer(1, lambda d: a_copy(1, d).start())
        rows = dot(unpack_ref[...], in_msg[wave].reshape(PEERS * MSG, SEG)).astype(jnp.bfloat16)
        for g in range(SEGS):
            xg[wave, own, :, pl.ds(g * SEG, SEG)] = rows[g * HALF : (g + 1) * HALF]

    def gather_1(wave):
        g_start(wave, 0, 1, 2, 3, 4, 5)

    def gather_2(wave):
        g_wait(wave, 0)
        g_start(wave, 6, 7)
        g_wait(wave, 1, 2)
        g_start(wave, 8, 9, 10, 11)

    def gather_3(wave):
        g_wait(wave, 3, 4)
        g_start(wave, 12, 13)
        g_wait(wave, 6, 7)
        g_start(wave, 14, 15)
        g_wait(wave, 8, 9)
        g_start(wave, 16, 17)

    def gather_4(wave):
        g_wait(wave, 5, 10, 11, 12, 13, 14, 15, 16, 17)

    def hidden(wave):
        rows = xg[wave].reshape(8 * HALF, D)
        units = lax.dot_general(rows, win[...], (((1,), (1,)), ((), ())), preferred_element_type=jnp.float32)
        hid[...] = jnp.maximum(units, 0.0).astype(jnp.bfloat16)

    def partial(wave, cols):
        part = dot(hid[...], wout[:, pl.ds(*cols)])
        pt[wave, :, :, pl.ds(*cols)] = part.astype(jnp.bfloat16).reshape(8, HALF, cols[1])

    def span(home, cols):
        return lambda wave: pt.at[wave, home, :, pl.ds(*cols)]

    def inner(buf, i, cols):
        return lambda wave: buf.at[wave, i, :, pl.ds(*cols)]

    sums = []
    for f in (1, 0):
        far = f == 1
        sums += [
            (span(blk(xo, far), PA), inner(r_p2r, f, PA), left),
            (span(blk(xo, far), PB), inner(r_p2l, f, PA), right),
            (span(blk(xl, far), PB), inner(r_pr, f, PB), left),
            (span(blk(xr, far), PA), inner(r_pl, f, PA), right),
            (span(blk(xl, far), PA), inner(r_pr, f, PA), left),
            (span(blk(xr, far), PB), inner(r_pl, f, PB), right),
        ]
    q0, q1 = (0, QA[1]), (QA[1], QB[1])
    sums += [
        (span(mate, PP), inner(r_py, 0, PP), across),
        (span(blk(xo, True), QQ), inner(r_qy, 0, (0, QQ[1])), across),
        (span(blk(xl, True), QQ), inner(r_qy, 1, (0, QQ[1])), across),
        (span(blk(xr, True), QQ), inner(r_qy, 2, (0, QQ[1])), across),
        (span(mate, QQ), inner(r_qy, 3, (0, QQ[1])), across),
        (span(blk(xo), QA), inner(r_q2r, 0, q0), left),
        (span(blk(xo), QB), inner(r_q2l, 0, q0), right),
        (span(blk(xl), QB), inner(r_qr, 0, q1), left),
        (span(blk(xr), QA), inner(r_ql, 0, q0), right),
        (span(blk(xl), QA), inner(r_qr, 0, q0), left),
        (span(blk(xr), QB), inner(r_ql, 0, q1), right),
    ]

    def s_copy(wave, i):
        src, dst, there = sums[i]
        return pltpu.make_async_remote_copy(
            src_ref=src(wave), dst_ref=dst(wave), send_sem=s_ssem.at[wave, i], recv_sem=s_rsem.at[wave, i],
            device_id=there, device_id_type=MESH,
        )

    def s_start(wave, *which):
        for i in which:
            s_copy(wave, i).start()

    def s_wait(wave, *which):
        for i in which:
            s_copy(wave, i).wait_recv()

    def add(wave, home, cols, *terms):
        step = 128

        @pl.loop(0, cols[1] // step)
        def _(i):
            here = pl.ds(pl.multiple_of(cols[0] + i * step, 128), step)
            total = pt[wave, home, :, here].astype(jnp.float32)
            for buf, j, first in terms:
                total += buf[wave, j, :, pl.ds(pl.multiple_of(first + i * step, 128), step)].astype(jnp.float32)
            pt[wave, home, :, here] = total.astype(jnp.bfloat16)

    def sum_p2(wave):
        for n, f in ((0, 1), (6, 0)):
            far = f == 1
            s_wait(wave, n, n + 1)
            add(wave, blk(xl, far), PA, (r_p2r, f, 0))
            s_start(wave, n + 4)
            add(wave, blk(xr, far), PB, (r_p2l, f, 0))
            s_start(wave, n + 5)

    def sum_p1(wave):
        for n, f in ((0, 1), (6, 0)):
            s_wait(wave, n + 2, n + 3, n + 4, n + 5)
            add(wave, blk(x, f == 1), PP, (r_pr, f, 0), (r_pl, f, 0))
            if f == 1:
                s_start(wave, 12)

    def sum_py(wave):
        s_wait(wave, 12)
        add(wave, own, PP, (r_py, 0, 0))

    def sum_qy(wave):
        s_wait(wave, 13)
        add(wave, blk(xo), QQ, (r_qy, 0, 0))
        s_start(wave, 17, 18)
        s_wait(wave, 14)
        add(wave, blk(xl), QQ, (r_qy, 1, 0))
        s_start(wave, 19)
        s_wait(wave, 15)
        add(wave, blk(xr), QQ, (r_qy, 2, 0))
        s_start(wave, 20)

    def sum_q2(wave):
        s_wait(wave, 17, 18)
        add(wave, blk(xl), QA, (r_q2r, 0, 0))
        s_start(wave, 21)
        add(wave, blk(xr), QB, (r_q2l, 0, 0))
        s_start(wave, 22)

    def sum_q1(wave):
        s_wait(wave, 16, 19, 20, 21, 22)
        add(wave, own, QQ, (r_qy, 3, 0), (r_qr, 0, 0), (r_ql, 0, 0))

    def send_back(wave):
        ret_msg[wave] = pack(pt[wave, own]).reshape(PEERS, MSG, SEG)
        each_peer(wave, lambda d: b_copy(wave, d).start())
        if wave == 0:
            self_b.start()

    def come_back(wave):
        if wave == 0:
            self_b.wait()
        each_peer(wave, lambda d: b_recv(wave, d).wait_recv())
        fin[wave] = dot(unpack_ref[...], ret_in[wave].reshape(PEERS * MSG, SEG)).astype(jnp.bfloat16)

    def partials(wave, send):
        partial(wave, PA)
        if send:
            s_start(wave, 0, 6, 3, 9)
        partial(wave, QA)
        partial(wave, QB)
        if send:
            s_start(wave, 13, 14, 15, 16)
        partial(wave, PB)
        if send:
            s_start(wave, 1, 7, 2, 8)

    def add_back(wave):
        for g in range(SEGS):
            cols = pl.ds(g * SEG, SEG)
            expert_out = dot(perm_t[:, wave * HALF : (wave + 1) * HALF], fin[wave, pl.ds(g * HALF, HALF)])
            mixed = state_ref[:, cols] + scale * expert_out
            if wave == 0:
                state_ref[:, cols] = mixed
            else:
                out_ref[0, :, cols] = mixed.astype(jnp.bfloat16)

    arrive(0)
    gather_1(0)
    gather_2(0)
    arrive(1)
    gather_3(0)
    gather_1(1)
    gather_4(0)
    for cp in w_local:
        cp.wait()
    for cp in w_swap:
        cp.wait_recv()
    hidden(0)
    gather_2(1)
    partials(0, False)
    gather_3(1)
    s_start(0, 0, 6, 3, 9, 13, 14, 15, 16, 1, 7, 2, 8)
    gather_4(1)
    hidden(1)
    sum_p2(0)
    sum_qy(0)
    partials(1, True)
    sum_p1(0)
    sum_q2(0)
    sum_p2(1)
    sum_py(0)
    sum_q1(0)
    send_back(0)
    sum_qy(1)
    sum_p1(1)
    sum_q2(1)
    come_back(0)
    add_back(0)
    sum_q1(1)
    sum_py(1)
    send_back(1)
    come_back(1)
    add_back(1)

    for i in range(4):
        k_copy(i).wait_send()
        neighbours(lambda: f_copy(i, True).wait_send(), lambda: f_copy(i, False).wait_send(), is_last, is_first)
        if i < RELAYED:
            pl.when(is_first)(lambda: relay_copy(i, True).wait_send())
            pl.when(is_last)(lambda: relay_copy(i, False).wait_send())
    for cp in w_swap:
        cp.wait_send()
    for wave in (0, 1):
        each_peer(wave, lambda d: a_recv(wave, d).wait_send())
        each_peer(wave, lambda d: b_recv(wave, d).wait_send())
        for i in range(len(gather)):
            g_copy(wave, i).wait_send()
        for i in range(len(sums)):
            s_copy(wave, i).wait_send()


def body(
    queries, dec_state, enc_kv, band_start, norm_gain, route_ids, keep, route_prob, w_in, w_out
):
    order = message_order()
    vmem = pl.BlockSpec(memory_space=pltpu.VMEM)
    hbm = pl.BlockSpec(memory_space=pl.ANY)
    bf = jnp.bfloat16
    return pl.pallas_call(
        moe_kernel,
        out_shape=jax.ShapeDtypeStruct((1, TOK, D), bf),
        in_specs=[pl.BlockSpec(memory_space=pltpu.SMEM)] + [vmem] * 4 + [hbm] * 7,
        out_specs=vmem,
        scratch_shapes=[
            pltpu.VMEM((SEGS * HALF, SEGS * HALF), bf),
            pltpu.VMEM((SEGS * HALF, SEGS * HALF), bf),
            pltpu.VMEM((TOK, D), bf),
            pltpu.VMEM((TOK, D), bf),
            pltpu.VMEM((TOK, D), jnp.float32),
            pltpu.VMEM((TOK, D), bf),
            pltpu.VMEM((2, 3, FR, KV_HEADS * DH), bf),
            pltpu.SemaphoreType.DMA((4,)),
            pltpu.SemaphoreType.DMA((4,)),
            pltpu.SemaphoreType.DMA((4,)),
            pltpu.SemaphoreType.DMA((4, 2)),
            pltpu.SemaphoreType.DMA((4, 2)),
            pltpu.SemaphoreType.DMA((2, 2)),
            pltpu.VMEM((2 * FS, D), bf),
            pltpu.VMEM((2 * FS, D), bf),
            pltpu.VMEM((8 * HALF, 2 * FS), bf),
            pltpu.VMEM((2, 8, HALF, D), bf),
            pltpu.VMEM((2, 8, HALF, D), bf),
            pltpu.VMEM((2, PEERS, MSG, SEG), bf),
            pltpu.VMEM((2, PEERS, MSG, SEG), bf),
            pltpu.VMEM((2, PEERS, MSG, SEG), bf),
            pltpu.VMEM((2, PEERS, MSG, SEG), bf),
            pltpu.VMEM((2, PEERS * MSG, SEG), bf),
            pltpu.VMEM((2, 2, HALF, PA[1]), bf),
            pltpu.VMEM((2, 2, HALF, PB[1]), bf),
            pltpu.VMEM((2, 2, HALF, PP[1]), bf),
            pltpu.VMEM((2, 2, HALF, PP[1]), bf),
            pltpu.VMEM((2, 1, HALF, PP[1]), bf),
            pltpu.VMEM((2, 4, HALF, QQ[1]), bf),
            pltpu.VMEM((2, 1, HALF, QA[1]), bf),
            pltpu.VMEM((2, 1, HALF, QB[1]), bf),
            pltpu.VMEM((2, 1, HALF, QQ[1]), bf),
            pltpu.VMEM((2, 1, HALF, QQ[1]), bf),
            pltpu.SemaphoreType.DMA((2,)),
            pltpu.SemaphoreType.DMA((2,)),
            pltpu.SemaphoreType.DMA((2,)),
            pltpu.SemaphoreType.DMA((2, PEERS)),
            pltpu.SemaphoreType.DMA((2, PEERS)),
            pltpu.SemaphoreType.DMA((2, PEERS)),
            pltpu.SemaphoreType.DMA((2, PEERS)),
            pltpu.SemaphoreType.DMA((2,)),
            pltpu.SemaphoreType.DMA((2, 18)),
            pltpu.SemaphoreType.DMA((2, 18)),
            pltpu.SemaphoreType.DMA((2, 23)),
            pltpu.SemaphoreType.DMA((2, 23)),
        ],
        compiler_params=pltpu.CompilerParams(
            collective_id=0, has_side_effects=True, vmem_limit_bytes=60 * 2**20
        ),
    )(
        band_start,
        route_ids.reshape(1, TOK),
        keep,
        route_prob,
        norm_gain.reshape(1, D),
        jnp.asarray(order, bf),
        jnp.asarray(order.T, bf),
        queries,
        dec_state,
        enc_kv,
        w_in,
        w_out,
    )


def solution(mesh):
    return jax.shard_map(
        body,
        mesh=mesh,
        in_specs=(
            P(("section", "expert"), "seq", None),
            P(("section", "expert"), "seq", None),
            P(None, ("section", "expert"), "seq", None),
            P(("section", "expert"), "seq"),
            P(),
            P(("section", "expert"), "seq", None),
            P(("section", "expert"), "seq"),
            P(("section", "expert"), "seq"),
            P("seq", ("section", "expert"), None),
            P("seq", ("section", "expert"), None),
        ),
        out_specs=P(("section", "expert"), "seq", None),
        check_vma=False,
    )
```

```python
import math

import jax
import jax.numpy as jnp
import numpy as np
from jax import lax
from jax.experimental import pallas as pl
from jax.experimental.pallas import tpu as pltpu
from jax.sharding import PartitionSpec as P

D = 4096
HEADS = 32
KV_HEADS = 8
DH = 128
WIN = 128
MESH = pl.DeviceIdType.MESH

TOK = 96
HALF = 48
SIDE = D // 2
SEGS = 8
SEG = SIDE // SEGS
MSG = 24
PEERS = 16
FS = 320
UNITS = 4
PA = (0, 640)
PB = (640, 512)
QA = (1152, 384)
QB = (1536, 512)
PP = (0, 1152)
QQ = (1152, 896)
FR = 160
KVC = 512
GROUP = HEADS // KV_HEADS


def message_order():
    order = np.zeros((SEGS * HALF, SEGS * HALF), np.float32)
    for seg in range(SEGS):
        for peer in range(PEERS):
            for j in range(3):
                order[seg * HALF + peer * 3 + j, peer * MSG + seg * 3 + j] = 1.0
    return order


def moe_kernel(
    first_ref, ids_ref, keep_ref, prob_ref, gain_ref,
    unpack_hbm, pack_hbm, queries_hbm, dec_hbm, kv_hbm, w_in_hbm, w_out_hbm,
    out_ref,
    unpack_ref, pack_ref, queries_ref, dec_ref, state_ref, normed_ref, kv,
    in_sem, k_ssem, k_rsem, f_ssem, f_rsem, x_ssem,
    win, wout, acc, hid, xg, pt, out_msg, in_msg, ret_msg, ret_in,
    r_p2r, r_p2l, r_pr, r_pl, r_py, r_qy, r_q2r, r_q2l, r_qr, r_ql,
    w_sem, wx_ssem, wx_rsem, a_ssem, a_rsem, b_ssem, b_rsem, self_sem, g_ssem, g_rsem, s_ssem, s_rsem,
):
    s = lax.axis_index("section")
    q = lax.axis_index("seq")
    x = lax.axis_index("expert")
    l, c = s // 2, s % 2
    yh, z = q // 8, q % 8
    me = z * 2 + c

    def dev(x_, l_, c_, yh_, z_):
        return (l_ * 2 + c_, yh_ * 8 + z_, x_)

    xr, xl, xo = (x + 1) % 4, (x + 3) % 4, (x + 2) % 4
    right, left = dev(xr, l, c, yh, z), dev(xl, l, c, yh, z)
    across, sibling = dev(x, 1 - l, c, yh, z), dev(x, l, 1 - c, yh, z)

    def peer(wave, d):
        if wave == 0:
            return dev(x, l, d % 2, yh, d // 2)
        return dev(x, 1 - l, d % 2, 1 - yh, d // 2)

    w_local = [
        pltpu.make_async_copy(w_in_hbm.at[c], win.at[pl.ds(0, FS)], w_sem.at[0]),
        pltpu.make_async_copy(w_out_hbm.at[c], wout.at[pl.ds(0, FS)], w_sem.at[1]),
    ]
    inputs = [
        pltpu.make_async_copy(src, dst, in_sem.at[i])
        for i, (src, dst) in enumerate(
            (
                (queries_hbm.at[0], queries_ref),
                (dec_hbm.at[0], dec_ref),
                (pack_hbm, pack_ref),
                (unpack_hbm, unpack_ref),
            )
        )
    ]

    barrier = pltpu.get_barrier_semaphore()
    corner = dev(x, 1 - l, 1 - c, yh, z)
    after, before = ((s, (q + 1) % 16, x), (s, (q + 15) % 16, x))
    opposite = dev(x, l, c, 1 - yh, z)
    for there in (corner, opposite, after, before, right, left, across):
        pl.semaphore_signal(barrier, inc=1, device_id=there, device_id_type=MESH)

    @pl.loop(1, PEERS)
    def _(i):
        pl.semaphore_signal(barrier, inc=1, device_id=peer(0, (me + i) % PEERS), device_id_type=MESH)

    @pl.loop(0, PEERS)
    def _(i):
        pl.semaphore_signal(barrier, inc=1, device_id=peer(1, (me + i) % PEERS), device_id_type=MESH)

    for cp in inputs:
        cp.start()
    for cp in w_local:
        cp.start()

    sub = lax.broadcasted_iota(jnp.int32, (TOK, TOK), 0)
    lane = lax.broadcasted_iota(jnp.int32, (TOK, TOK), 1)

    def column(row):
        return jnp.sum(jnp.where(sub == lane, row, 0.0), axis=1, keepdims=True)

    ids_r = ids_ref[...].astype(jnp.float32)
    ids_c = column(ids_r)
    scale = column(keep_ref[...].astype(jnp.float32) * prob_ref[...])
    same = ids_c == ids_r
    rank_c = jnp.sum(jnp.where(same & (lane < sub), 1.0, 0.0), axis=1, keepdims=True)
    rank_r = jnp.sum(jnp.where(same & (sub < lane), 1.0, 0.0), axis=0, keepdims=True)

    def slot(ids, rank):
        hi = jnp.where(ids >= PEERS, 1.0, 0.0)
        here = yh.astype(jnp.float32)
        wave = hi + here - 2.0 * hi * here
        return (wave * PEERS + ids - hi * PEERS) * 3.0 + rank

    perm = (slot(ids_r, rank_r) == sub.astype(jnp.float32)).astype(jnp.bfloat16)
    perm_t = (slot(ids_c, rank_c) == lane.astype(jnp.float32)).astype(jnp.bfloat16)

    def dot(a, b):
        return jnp.dot(a, b, preferred_element_type=jnp.float32)

    def pack(rows):
        return dot(pack_ref[...], jnp.concatenate([rows[:, g * SEG : (g + 1) * SEG] for g in range(SEGS)], axis=0)).astype(jnp.bfloat16)

    def a_copy(u, d):
        return pltpu.make_async_remote_copy(
            src_ref=out_msg.at[u, d], dst_ref=in_msg.at[u, me],
            send_sem=a_ssem.at[u, d], recv_sem=a_rsem.at[u, me],
            device_id=peer(u // 2, d), device_id_type=MESH,
        )

    def a_recv(u, d):
        return pltpu.make_async_remote_copy(
            src_ref=out_msg.at[u, d], dst_ref=in_msg.at[u, d],
            send_sem=a_ssem.at[u, d], recv_sem=a_rsem.at[u, d],
            device_id=peer(u // 2, d), device_id_type=MESH,
        )

    def b_copy(u, d):
        return pltpu.make_async_remote_copy(
            src_ref=ret_msg.at[u, d], dst_ref=ret_in.at[u, me],
            send_sem=b_ssem.at[u, d], recv_sem=b_rsem.at[u, me],
            device_id=peer(u // 2, d), device_id_type=MESH,
        )

    def b_recv(u, d):
        return pltpu.make_async_remote_copy(
            src_ref=ret_msg.at[u, d], dst_ref=ret_in.at[u, d],
            send_sem=b_ssem.at[u, d], recv_sem=b_rsem.at[u, d],
            device_id=peer(u // 2, d), device_id_type=MESH,
        )

    def each_peer(u, act):
        @pl.loop(1 if u < 2 else 0, PEERS)
        def _(i):
            act((me + i) % PEERS)

    self_a = [pltpu.make_async_copy(out_msg.at[u, me], in_msg.at[u, me], self_sem.at[u]) for u in (0, 1)]
    self_b = [pltpu.make_async_copy(ret_msg.at[u, me], ret_in.at[u, me], self_sem.at[2 + u]) for u in (0, 1)]

    def a_start(u):
        each_peer(u, lambda d: a_copy(u, d).start())
        if u < 2:
            self_a[u].start()

    def outgoing(wave):
        rows = dot(perm[wave * HALF : (wave + 1) * HALF], normed_ref[...]).astype(jnp.bfloat16)
        for side in (0, 1):
            out_msg[2 * wave + side] = pack(rows[:, side * SIDE : (side + 1) * SIDE]).reshape(PEERS, MSG, SEG)

    nxt = ((s + 1) % 4, q, x)

    def chunk(i):
        return i % 2, pl.ds((i // 2) * KVC, KVC)

    def k_copy(i):
        which, cols = chunk(i)
        return pltpu.make_async_remote_copy(
            src_ref=kv_hbm.at[which, 0, :, cols], dst_ref=kv.at[which, 1, :, cols],
            send_sem=k_ssem.at[i], recv_sem=k_rsem.at[i], device_id=nxt, device_id_type=MESH,
        )

    RELAYED = 2
    ring_after, ring_before = dev(x, l, c, yh, (z + 1) % 8), dev(x, l, c, yh, (z + 7) % 8)

    def f_copy(i, up):
        which, cols = chunk(i)
        to = 0 if up else 2
        if i < RELAYED:
            there = ring_after if up else ring_before
        else:
            there = after if up else before
        return pltpu.make_async_remote_copy(
            src_ref=kv.at[which, 1, :, cols], dst_ref=kv.at[which, to, :, cols],
            send_sem=f_ssem.at[i, to // 2], recv_sem=f_rsem.at[i, to // 2],
            device_id=there, device_id_type=MESH,
        )

    def relay_copy(i, up):
        which, cols = chunk(i)
        to = 0 if up else 2
        return pltpu.make_async_remote_copy(
            src_ref=kv.at[which, to, :, cols], dst_ref=kv.at[which, to, :, cols],
            send_sem=x_ssem.at[i, to // 2], recv_sem=f_rsem.at[i, to // 2],
            device_id=opposite, device_id_type=MESH,
        )

    is_first, is_last = q == 0, q == 15

    def relay(i):
        for edge, up in ((is_first, True), (is_last, False)):

            @pl.when(edge)
            def _():
                f_copy(i, up).wait_recv()
                relay_copy(i, up).start()

    for edge, to in ((is_first, 0), (is_last, 2)):

        @pl.when(edge)
        def _():
            for which in (0, 1):
                kv[which, to, :, pl.ds(KVC, KVC)] = jnp.zeros((FR, KVC), jnp.bfloat16)

    def neighbours(act_up, act_down, up_edge, down_edge):
        pl.when(jnp.logical_not(up_edge))(act_up)
        pl.when(jnp.logical_not(down_edge))(act_down)

    pl.semaphore_wait(barrier, 38)
    for i in range(4):
        k_copy(i).start()
    for i in range(4):
        k_copy(i).wait_recv()
        neighbours(lambda: f_copy(i, True).start(), lambda: f_copy(i, False).start(), is_last, is_first)
        if 1 <= i <= RELAYED:
            relay(i - 1)

    w_swap = [
        pltpu.make_async_remote_copy(
            src_ref=hbm.at[1 - c], dst_ref=vmem.at[pl.ds(FS, FS)], send_sem=wx_ssem.at[i], recv_sem=wx_rsem.at[i],
            device_id=sibling, device_id_type=MESH,
        )
        for i, (hbm, vmem) in enumerate(((w_in_hbm, win), (w_out_hbm, wout)))
    ]
    for cp in w_swap:
        cp.start()

    for cp in inputs:
        cp.wait()
    first = first_ref[0, 0] - (q - 1) * FR
    frame = lax.broadcasted_iota(jnp.int32, (WIN, 3 * FR), 1)
    row = lax.broadcasted_iota(jnp.int32, (WIN, 3 * FR), 0)
    band = jnp.where(frame == row + first, 1.0, 0.0).astype(jnp.bfloat16)
    squares = jnp.zeros((TOK, DH), jnp.float32)
    for part in (0, 1):
        for i in (2 * part, 2 * part + 1):
            neighbours(
                lambda: f_copy(i, True).wait_recv(), lambda: f_copy(i, False).wait_recv(), is_first, is_last
            )
        part_cols = pl.ds(part * KVC, KVC)
        keys, values = (
            dot(band, kv[which, :, :, part_cols].reshape(3 * FR, KVC)).astype(jnp.bfloat16) for which in (0, 1)
        )
        for h in range(KV_HEADS // 2):
            at = slice(h * DH, (h + 1) * DH)
            heads = [pl.ds(((part * 4 + h) * GROUP + g) * DH, DH) for g in range(GROUP)]
            rows = jnp.concatenate([queries_ref[:, cols] for cols in heads], axis=0)
            scores = lax.dot_general(
                rows, keys[:, at], (((1,), (1,)), ((), ())), preferred_element_type=jnp.float32
            ) * (1.0 / math.sqrt(DH))
            weights = jnp.exp(scores - jnp.max(scores, axis=1, keepdims=True))
            total = jnp.sum(weights, axis=1, keepdims=True)
            context = dot(weights.astype(jnp.bfloat16), values[:, at]) / total
            for g, cols in enumerate(heads):
                state = dec_ref[:, cols].astype(jnp.float32) + context[g * TOK : (g + 1) * TOK]
                state_ref[:, cols] = state
                squares += state * state
    inverse = lax.rsqrt(jnp.sum(squares, axis=1, keepdims=True) * (1.0 / D) + 1e-06)
    for h in range(HEADS):
        cols = pl.ds(h * DH, DH)
        normed_ref[:, cols] = (state_ref[:, cols] * inverse * gain_ref[:, cols]).astype(jnp.bfloat16)

    outgoing(0)
    a_start(0)

    own, mate = x * 2 + l, x * 2 + 1 - l

    def blk(x_, far=False):
        return x_ * 2 + (1 - l if far else l)

    gather = [
        (own, PP, across, mate),
        (own, QQ, right, blk(xl)),
        (own, QQ, left, blk(xr)),
        (own, PP, right, blk(xl)),
        (own, PP, left, blk(xr)),
        (own, QQ, across, mate),
        (mate, PP, right, blk(xl, True)),
        (mate, PP, left, blk(xr, True)),
        (blk(xl), QA, right, blk(xo)),
        (blk(xr), QB, left, blk(xo)),
        (blk(xl), QQ, across, blk(xl, True)),
        (blk(xr), QQ, across, blk(xr, True)),
        (blk(xl), PA, right, blk(xo)),
        (blk(xr), PB, left, blk(xo)),
        (blk(xl, True), PA, right, blk(xo, True)),
        (blk(xr, True), PB, left, blk(xo, True)),
        (blk(xo), QA, across, blk(xo, True)),
        (blk(xo), QB, across, blk(xo, True)),
    ]

    def wide(u, cols):
        return pl.ds((u % 2) * SIDE + cols[0], cols[1])

    def g_copy(u, i, received=False):
        sent, cols, there, got = gather[i]
        ref = xg.at[u // 2, got if received else sent, :, wide(u, cols)]
        return pltpu.make_async_remote_copy(
            src_ref=ref, dst_ref=ref, send_sem=g_ssem.at[u, i], recv_sem=g_rsem.at[u, i],
            device_id=there, device_id_type=MESH,
        )

    def g_start(wave, *which):
        for i in which:
            g_copy(wave, i).start()

    def g_wait(wave, *which):
        for i in which:
            g_copy(wave, i, True).wait_recv()

    def arrive(u):
        if u < 2:
            self_a[u].wait()
        each_peer(u, lambda d: a_recv(u, d).wait_recv())
        rows = dot(unpack_ref[...], in_msg[u].reshape(PEERS * MSG, SEG)).astype(jnp.bfloat16)
        for g in range(SEGS):
            xg[u // 2, own, :, wide(u, (g * SEG, SEG))] = rows[g * HALF : (g + 1) * HALF]

    def gather_1(wave):
        g_start(wave, 0, 1, 2, 3, 4, 5)

    def hand_on(u, received, then):
        g_wait(u, *received)
        g_start(u, *then)

    def gather_4(wave):
        g_wait(wave, 5, 10, 11, 12, 13, 14, 15, 16, 17)

    def hidden(u):
        rows = xg[u // 2, :, :, wide(u, (0, SIDE))].reshape(8 * HALF, SIDE)
        units = lax.dot_general(
            rows, win[:, wide(u, (0, SIDE))], (((1,), (1,)), ((), ())), preferred_element_type=jnp.float32
        )
        if u % 2 == 0:
            acc[...] = units
        else:
            hid[...] = jnp.maximum(acc[...] + units, 0.0).astype(jnp.bfloat16)

    def partial(u):
        for cols in (PA, QQ, PB):
            part = dot(hid[...], wout[:, wide(u, cols)])
            pt[u // 2, :, :, wide(u, cols)] = part.astype(jnp.bfloat16).reshape(8, HALF, cols[1])

    def span(home, cols):
        return lambda u: pt.at[u // 2, home, :, wide(u, cols)]

    def inner(buf, i, cols):
        return lambda u: buf.at[u, i, :, pl.ds(*cols)]

    sums = []
    for f in (1, 0):
        far = f == 1
        sums += [
            (span(blk(xo, far), PA), inner(r_p2r, f, PA), left),
            (span(blk(xo, far), PB), inner(r_p2l, f, (0, PB[1])), right),
            (span(blk(xl, far), PB), inner(r_pr, f, PB), left),
            (span(blk(xr, far), PA), inner(r_pl, f, PA), right),
            (span(blk(xl, far), PA), inner(r_pr, f, PA), left),
            (span(blk(xr, far), PB), inner(r_pl, f, PB), right),
        ]
    q0, q1 = (0, QA[1]), (QA[1], QB[1])
    sums += [
        (span(mate, PP), inner(r_py, 0, PP), across),
        (span(blk(xo, True), QQ), inner(r_qy, 0, (0, QQ[1])), across),
        (span(blk(xl, True), QQ), inner(r_qy, 1, (0, QQ[1])), across),
        (span(blk(xr, True), QQ), inner(r_qy, 2, (0, QQ[1])), across),
        (span(mate, QQ), inner(r_qy, 3, (0, QQ[1])), across),
        (span(blk(xo), QA), inner(r_q2r, 0, q0), left),
        (span(blk(xo), QB), inner(r_q2l, 0, (0, QB[1])), right),
        (span(blk(xl), QB), inner(r_qr, 0, q1), left),
        (span(blk(xr), QA), inner(r_ql, 0, q0), right),
        (span(blk(xl), QA), inner(r_qr, 0, q0), left),
        (span(blk(xr), QB), inner(r_ql, 0, q1), right),
    ]

    def s_copy(wave, i):
        src, dst, there = sums[i]
        return pltpu.make_async_remote_copy(
            src_ref=src(wave), dst_ref=dst(wave), send_sem=s_ssem.at[wave, i], recv_sem=s_rsem.at[wave, i],
            device_id=there, device_id_type=MESH,
        )

    def s_start(wave, *which):
        for i in which:
            s_copy(wave, i).start()

    def s_wait(wave, *which):
        for i in which:
            s_copy(wave, i).wait_recv()

    def add(u, home, cols, *terms):
        step = 128

        @pl.loop(0, cols[1] // step)
        def _(i):
            here = pl.ds(pl.multiple_of((u % 2) * SIDE + cols[0] + i * step, 128), step)
            total = pt[u // 2, home, :, here].astype(jnp.float32)
            for buf, j in terms:
                total += buf[u, j, :, pl.ds(pl.multiple_of(i * step, 128), step)].astype(jnp.float32)
            pt[u // 2, home, :, here] = total.astype(jnp.bfloat16)

    def sum_p2(u, f):
        n, far = (0, True) if f == 1 else (6, False)
        s_wait(u, n, n + 1)
        add(u, blk(xl, far), PA, (r_p2r, f))
        s_start(u, n + 4)
        add(u, blk(xr, far), PB, (r_p2l, f))
        s_start(u, n + 5)

    def sum_p1(u, f):
        n, far = (0, True) if f == 1 else (6, False)
        s_wait(u, n + 2, n + 3, n + 4, n + 5)
        add(u, blk(x, far), PP, (r_pr, f), (r_pl, f))
        if far:
            s_start(u, 12)

    def sum_py(u):
        s_wait(u, 12)
        add(u, own, PP, (r_py, 0))

    def sum_qy(u, i):
        s_wait(u, 13 + i)
        add(u, blk((xo, xl, xr)[i]), QQ, (r_qy, i))
        s_start(u, *((17, 18), (19,), (20,))[i])

    def sum_q2(u):
        s_wait(u, 17, 18)
        add(u, blk(xl), QA, (r_q2r, 0))
        s_start(u, 21)
        add(u, blk(xr), QB, (r_q2l, 0))
        s_start(u, 22)

    def sum_q1(u):
        s_wait(u, 16, 19, 20, 21, 22)
        add(u, own, QQ, (r_qy, 3), (r_qr, 0), (r_ql, 0))

    def send_back(u):
        ret_msg[u] = pack(pt[u // 2, own, :, wide(u, (0, SIDE))]).reshape(PEERS, MSG, SEG)
        each_peer(u, lambda d: b_copy(u, d).start())
        if u < 2:
            self_b[u].start()

    def come_back(u):
        if u < 2:
            self_b[u].wait()
        each_peer(u, lambda d: b_recv(u, d).wait_recv())
        wave = u // 2
        rows = dot(unpack_ref[...], ret_in[u].reshape(PEERS * MSG, SEG)).astype(jnp.bfloat16)
        for g in range(SEGS):
            cols = wide(u, (g * SEG, SEG))
            expert_out = dot(perm_t[:, wave * HALF : (wave + 1) * HALF], rows[g * HALF : (g + 1) * HALF])
            mixed = state_ref[:, cols] + scale * expert_out
            if wave == 0:
                state_ref[:, cols] = mixed
            else:
                out_ref[0, :, cols] = mixed.astype(jnp.bfloat16)

    def sums_start(u):
        s_start(u, 0, 6, 1, 7, 13, 14, 15, 16, 3, 9, 2, 8)

    def sent(u, *kinds):
        for kind in kinds:
            if kind == "a":
                each_peer(u, lambda d: a_recv(u, d).wait_send())
            if kind == "g":
                for i in range(len(gather)):
                    g_copy(u, i).wait_send()
            if kind == "s":
                for i in range(len(sums)):
                    s_copy(u, i).wait_send()
            if kind == "b":
                each_peer(u, lambda d: b_recv(u, d).wait_send())

    a_start(1)
    outgoing(1)
    arrive(0)
    gather_1(0)
    a_start(2)
    arrive(1)
    gather_1(1)
    hand_on(0, (1, 2), (8, 9, 10, 11))
    a_start(3)
    hand_on(0, (0,), (6, 7))
    hand_on(0, (3, 4), (12, 13))
    arrive(2)
    hand_on(1, (0,), (6, 7))
    hand_on(1, (1, 2), (8, 9, 10, 11))
    gather_1(2)
    hand_on(1, (3, 4), (12, 13))
    hand_on(0, (8, 9), (16, 17))
    arrive(3)
    gather_1(3)
    hand_on(0, (6, 7), (14, 15))
    hand_on(1, (6, 7), (14, 15))
    hand_on(1, (8, 9), (16, 17))
    hand_on(2, (0,), (6, 7))
    hand_on(2, (1, 2), (8, 9, 10, 11))
    hand_on(2, (3, 4), (12, 13))
    hand_on(3, (1, 2), (8, 9, 10, 11))
    hand_on(3, (0,), (6, 7))
    hand_on(3, (3, 4), (12, 13))
    gather_4(0)
    for cp in w_local:
        cp.wait()
    for cp in w_swap:
        cp.wait_recv()
    hidden(0)
    gather_4(1)
    hidden(1)
    partial(1)
    hand_on(2, (8, 9), (16, 17))
    partial(0)
    sums_start(0)
    hand_on(3, (8, 9), (16, 17))
    hand_on(2, (6, 7), (14, 15))
    sums_start(1)
    hand_on(3, (6, 7), (14, 15))
    sum_p2(0, 1)
    sum_qy(0, 0)
    sum_p2(0, 0)
    sum_qy(0, 1)
    sum_qy(0, 2)
    gather_4(2)
    hidden(2)
    sum_p2(1, 1)
    sum_p2(1, 0)
    sum_qy(1, 0)
    gather_4(3)
    hidden(3)
    sum_p1(0, 1)
    sum_q2(0)
    partial(2)
    sums_start(2)
    sum_p1(0, 0)
    sum_p1(1, 1)
    partial(3)
    sum_p1(1, 0)
    sum_py(0)
    sum_q1(0)
    sum_qy(2, 0)
    sum_p2(2, 1)
    sums_start(3)
    send_back(0)
    sent(0, "a", "g")
    sum_qy(2, 2)
    sum_qy(1, 1)
    sum_qy(2, 1)
    sum_qy(1, 2)
    sum_q2(1)
    sum_q2(2)
    sum_p2(2, 0)
    sum_p1(2, 1)
    sum_p2(3, 1)
    sum_py(1)
    sum_p2(3, 0)
    come_back(0)
    sum_qy(3, 0)
    sum_qy(3, 1)
    sum_qy(3, 2)
    sum_q1(1)
    send_back(1)
    sum_q1(2)
    sum_p1(2, 0)
    sum_p1(3, 1)
    sum_py(2)
    send_back(2)
    sum_q2(3)
    sent(2, "a", "g")
    sum_p1(3, 0)
    sent(1, "a", "g")
    sum_py(3)
    sum_q1(3)
    send_back(3)
    sent(3, "a", "g")
    come_back(1)
    come_back(2)
    come_back(3)
    for u in range(UNITS):
        sent(u, "s", "b")

    for i in range(4):
        k_copy(i).wait_send()
        neighbours(lambda: f_copy(i, True).wait_send(), lambda: f_copy(i, False).wait_send(), is_last, is_first)
        if i < RELAYED:
            pl.when(is_first)(lambda: relay_copy(i, True).wait_send())
            pl.when(is_last)(lambda: relay_copy(i, False).wait_send())
    for cp in w_swap:
        cp.wait_send()


def body(
    queries, dec_state, enc_kv, band_start, norm_gain, route_ids, keep, route_prob, w_in, w_out
):
    order = message_order()
    vmem = pl.BlockSpec(memory_space=pltpu.VMEM)
    hbm = pl.BlockSpec(memory_space=pl.ANY)
    bf = jnp.bfloat16
    return pl.pallas_call(
        moe_kernel,
        out_shape=jax.ShapeDtypeStruct((1, TOK, D), bf),
        in_specs=[pl.BlockSpec(memory_space=pltpu.SMEM)] + [vmem] * 4 + [hbm] * 7,
        out_specs=vmem,
        scratch_shapes=[
            pltpu.VMEM((SEGS * HALF, SEGS * HALF), bf),
            pltpu.VMEM((SEGS * HALF, SEGS * HALF), bf),
            pltpu.VMEM((TOK, D), bf),
            pltpu.VMEM((TOK, D), bf),
            pltpu.VMEM((TOK, D), jnp.float32),
            pltpu.VMEM((TOK, D), bf),
            pltpu.VMEM((2, 3, FR, KV_HEADS * DH), bf),
            pltpu.SemaphoreType.DMA((4,)),
            pltpu.SemaphoreType.DMA((4,)),
            pltpu.SemaphoreType.DMA((4,)),
            pltpu.SemaphoreType.DMA((4, 2)),
            pltpu.SemaphoreType.DMA((4, 2)),
            pltpu.SemaphoreType.DMA((2, 2)),
            pltpu.VMEM((2 * FS, D), bf),
            pltpu.VMEM((2 * FS, D), bf),
            pltpu.VMEM((8 * HALF, 2 * FS), jnp.float32),
            pltpu.VMEM((8 * HALF, 2 * FS), bf),
            pltpu.VMEM((2, 8, HALF, D), bf),
            pltpu.VMEM((2, 8, HALF, D), bf),
            pltpu.VMEM((UNITS, PEERS, MSG, SEG), bf),
            pltpu.VMEM((UNITS, PEERS, MSG, SEG), bf),
            pltpu.VMEM((UNITS, PEERS, MSG, SEG), bf),
            pltpu.VMEM((UNITS, PEERS, MSG, SEG), bf),
            pltpu.VMEM((UNITS, 2, HALF, PA[1]), bf),
            pltpu.VMEM((UNITS, 2, HALF, PB[1]), bf),
            pltpu.VMEM((UNITS, 2, HALF, PP[1]), bf),
            pltpu.VMEM((UNITS, 2, HALF, PP[1]), bf),
            pltpu.VMEM((UNITS, 1, HALF, PP[1]), bf),
            pltpu.VMEM((UNITS, 4, HALF, QQ[1]), bf),
            pltpu.VMEM((UNITS, 1, HALF, QA[1]), bf),
            pltpu.VMEM((UNITS, 1, HALF, QB[1]), bf),
            pltpu.VMEM((UNITS, 1, HALF, QQ[1]), bf),
            pltpu.VMEM((UNITS, 1, HALF, QQ[1]), bf),
            pltpu.SemaphoreType.DMA((2,)),
            pltpu.SemaphoreType.DMA((2,)),
            pltpu.SemaphoreType.DMA((2,)),
            pltpu.SemaphoreType.DMA((UNITS, PEERS)),
            pltpu.SemaphoreType.DMA((UNITS, PEERS)),
            pltpu.SemaphoreType.DMA((UNITS, PEERS)),
            pltpu.SemaphoreType.DMA((UNITS, PEERS)),
            pltpu.SemaphoreType.DMA((4,)),
            pltpu.SemaphoreType.DMA((UNITS, 18)),
            pltpu.SemaphoreType.DMA((UNITS, 18)),
            pltpu.SemaphoreType.DMA((UNITS, 23)),
            pltpu.SemaphoreType.DMA((UNITS, 23)),
        ],
        compiler_params=pltpu.CompilerParams(
            collective_id=0, has_side_effects=True, vmem_limit_bytes=60 * 2**20
        ),
    )(
        band_start,
        route_ids.reshape(1, TOK),
        keep,
        route_prob,
        norm_gain.reshape(1, D),
        jnp.asarray(order, bf),
        jnp.asarray(order.T, bf),
        queries,
        dec_state,
        enc_kv,
        w_in,
        w_out,
    )


def solution(mesh):
    return jax.shard_map(
        body,
        mesh=mesh,
        in_specs=(
            P(("section", "expert"), "seq", None),
            P(("section", "expert"), "seq", None),
            P(None, ("section", "expert"), "seq", None),
            P(("section", "expert"), "seq"),
            P(),
            P(("section", "expert"), "seq", None),
            P(("section", "expert"), "seq"),
            P(("section", "expert"), "seq"),
            P("seq", ("section", "expert"), None),
            P("seq", ("section", "expert"), None),
        ),
        out_specs=P(("section", "expert"), "seq", None),
        check_vma=False,
    )
```

```python
import math

import jax
import jax.numpy as jnp
import numpy as np
from jax import lax
from jax.experimental import pallas as pl
from jax.experimental.pallas import tpu as pltpu
from jax.sharding import PartitionSpec as P

D = 4096
HEADS = 32
KV_HEADS = 8
DH = 128
WIN = 128
MESH = pl.DeviceIdType.MESH

TOK = 96
HALF = 48
SIDE = D // 2
SEGS = 8
SEG = SIDE // SEGS
MSG = 24
PEERS = 16
FS = 320
UNITS = 4
PA = (0, 640)
PB = (640, 512)
QA = (1152, 384)
QB = (1536, 512)
PP = (0, 1152)
QQ = (1152, 896)
FR = 160
KVC = 512
GROUP = HEADS // KV_HEADS


def message_order():
    order = np.zeros((SEGS * HALF, SEGS * HALF), np.float32)
    for seg in range(SEGS):
        for peer in range(PEERS):
            for j in range(3):
                order[seg * HALF + peer * 3 + j, peer * MSG + seg * 3 + j] = 1.0
    return order


def moe_kernel(
    first_ref, ids_ref, keep_ref, prob_ref, gain_ref,
    unpack_hbm, pack_hbm, queries_hbm, dec_hbm, kv_hbm, w_in_hbm, w_out_hbm,
    out_ref,
    unpack_ref, pack_ref, queries_ref, dec_ref, state_ref, normed_ref, kv,
    in_sem, k_ssem, k_rsem, f_ssem, f_rsem, x_ssem,
    win, wout, acc, hid, xg, pt, out_msg, in_msg, ret_msg, ret_in,
    r_p2r, r_p2l, r_pr, r_pl, r_py, r_qy, r_q2r, r_q2l, r_qr, r_ql,
    w_sem, wx_ssem, wx_rsem, a_ssem, a_rsem, b_ssem, b_rsem, self_sem, g_ssem, g_rsem, s_ssem, s_rsem,
):
    s = lax.axis_index("section")
    q = lax.axis_index("seq")
    x = lax.axis_index("expert")
    l, c = s // 2, s % 2
    yh, z = q // 8, q % 8
    me = z * 2 + c

    def dev(x_, l_, c_, yh_, z_):
        return (l_ * 2 + c_, yh_ * 8 + z_, x_)

    xr, xl, xo = (x + 1) % 4, (x + 3) % 4, (x + 2) % 4
    right, left = dev(xr, l, c, yh, z), dev(xl, l, c, yh, z)
    across, sibling = dev(x, 1 - l, c, yh, z), dev(x, l, 1 - c, yh, z)

    def peer(wave, d):
        if wave == 0:
            return dev(x, l, d % 2, yh, d // 2)
        return dev(x, 1 - l, d % 2, 1 - yh, d // 2)

    w_local = [
        pltpu.make_async_copy(w_in_hbm.at[c], win.at[pl.ds(0, FS)], w_sem.at[0]),
        pltpu.make_async_copy(w_out_hbm.at[c], wout.at[pl.ds(0, FS)], w_sem.at[1]),
    ]
    inputs = [
        pltpu.make_async_copy(src, dst, in_sem.at[i])
        for i, (src, dst) in enumerate(
            (
                (queries_hbm.at[0], queries_ref),
                (dec_hbm.at[0], dec_ref),
                (pack_hbm, pack_ref),
                (unpack_hbm, unpack_ref),
            )
        )
    ]

    barrier = pltpu.get_barrier_semaphore()
    corner = dev(x, 1 - l, 1 - c, yh, z)
    after, before = ((s, (q + 1) % 16, x), (s, (q + 15) % 16, x))
    opposite = dev(x, l, c, 1 - yh, z)
    for there in (corner, opposite, after, before, right, left, across):
        pl.semaphore_signal(barrier, inc=1, device_id=there, device_id_type=MESH)

    @pl.loop(1, PEERS)
    def _(i):
        pl.semaphore_signal(barrier, inc=1, device_id=peer(0, (me + i) % PEERS), device_id_type=MESH)

    @pl.loop(0, PEERS)
    def _(i):
        pl.semaphore_signal(barrier, inc=1, device_id=peer(1, (me + i) % PEERS), device_id_type=MESH)

    for cp in inputs:
        cp.start()
    for cp in w_local:
        cp.start()

    sub = lax.broadcasted_iota(jnp.int32, (TOK, TOK), 0)
    lane = lax.broadcasted_iota(jnp.int32, (TOK, TOK), 1)

    def column(row):
        return jnp.sum(jnp.where(sub == lane, row, 0.0), axis=1, keepdims=True)

    ids_r = ids_ref[...].astype(jnp.float32)
    ids_c = column(ids_r)
    scale = column(keep_ref[...].astype(jnp.float32) * prob_ref[...])
    same = ids_c == ids_r
    rank_c = jnp.sum(jnp.where(same & (lane < sub), 1.0, 0.0), axis=1, keepdims=True)
    rank_r = jnp.sum(jnp.where(same & (sub < lane), 1.0, 0.0), axis=0, keepdims=True)

    def slot(ids, rank):
        hi = jnp.where(ids >= PEERS, 1.0, 0.0)
        here = yh.astype(jnp.float32)
        wave = hi + here - 2.0 * hi * here
        return (wave * PEERS + ids - hi * PEERS) * 3.0 + rank

    perm = (slot(ids_r, rank_r) == sub.astype(jnp.float32)).astype(jnp.bfloat16)
    perm_t = (slot(ids_c, rank_c) == lane.astype(jnp.float32)).astype(jnp.bfloat16)

    def dot(a, b):
        return jnp.dot(a, b, preferred_element_type=jnp.float32)

    def pack(rows):
        return dot(pack_ref[...], jnp.concatenate([rows[:, g * SEG : (g + 1) * SEG] for g in range(SEGS)], axis=0)).astype(jnp.bfloat16)

    def a_copy(u, d):
        return pltpu.make_async_remote_copy(
            src_ref=out_msg.at[u, d], dst_ref=in_msg.at[u, me],
            send_sem=a_ssem.at[u, d], recv_sem=a_rsem.at[u, me],
            device_id=peer(u // 2, d), device_id_type=MESH,
        )

    def a_recv(u, d):
        return pltpu.make_async_remote_copy(
            src_ref=out_msg.at[u, d], dst_ref=in_msg.at[u, d],
            send_sem=a_ssem.at[u, d], recv_sem=a_rsem.at[u, d],
            device_id=peer(u // 2, d), device_id_type=MESH,
        )

    def b_copy(u, d):
        return pltpu.make_async_remote_copy(
            src_ref=ret_msg.at[u, d], dst_ref=ret_in.at[u, me],
            send_sem=b_ssem.at[u, d], recv_sem=b_rsem.at[u, me],
            device_id=peer(u // 2, d), device_id_type=MESH,
        )

    def b_recv(u, d):
        return pltpu.make_async_remote_copy(
            src_ref=ret_msg.at[u, d], dst_ref=ret_in.at[u, d],
            send_sem=b_ssem.at[u, d], recv_sem=b_rsem.at[u, d],
            device_id=peer(u // 2, d), device_id_type=MESH,
        )

    def each_peer(u, act):
        @pl.loop(1 if u < 2 else 0, PEERS)
        def _(i):
            act((me + i) % PEERS)

    self_a = [pltpu.make_async_copy(out_msg.at[u, me], in_msg.at[u, me], self_sem.at[u]) for u in (0, 1)]
    self_b = [pltpu.make_async_copy(ret_msg.at[u, me], ret_in.at[u, me], self_sem.at[2 + u]) for u in (0, 1)]

    def a_start(u):
        each_peer(u, lambda d: a_copy(u, d).start())
        if u < 2:
            self_a[u].start()

    def outgoing(wave):
        rows = dot(perm[wave * HALF : (wave + 1) * HALF], normed_ref[...]).astype(jnp.bfloat16)
        for side in (0, 1):
            out_msg[2 * wave + side] = pack(rows[:, side * SIDE : (side + 1) * SIDE]).reshape(PEERS, MSG, SEG)

    nxt = ((s + 1) % 4, q, x)

    def chunk(i):
        return i % 2, pl.ds((i // 2) * KVC, KVC)

    def k_copy(i):
        which, cols = chunk(i)
        return pltpu.make_async_remote_copy(
            src_ref=kv_hbm.at[which, 0, :, cols], dst_ref=kv.at[which, 1, :, cols],
            send_sem=k_ssem.at[i], recv_sem=k_rsem.at[i], device_id=nxt, device_id_type=MESH,
        )

    RELAYED = 2
    ring_after, ring_before = dev(x, l, c, yh, (z + 1) % 8), dev(x, l, c, yh, (z + 7) % 8)

    def f_copy(i, up):
        which, cols = chunk(i)
        to = 0 if up else 2
        if i < RELAYED:
            there = ring_after if up else ring_before
        else:
            there = after if up else before
        return pltpu.make_async_remote_copy(
            src_ref=kv.at[which, 1, :, cols], dst_ref=kv.at[which, to, :, cols],
            send_sem=f_ssem.at[i, to // 2], recv_sem=f_rsem.at[i, to // 2],
            device_id=there, device_id_type=MESH,
        )

    def relay_copy(i, up):
        which, cols = chunk(i)
        to = 0 if up else 2
        return pltpu.make_async_remote_copy(
            src_ref=kv.at[which, to, :, cols], dst_ref=kv.at[which, to, :, cols],
            send_sem=x_ssem.at[i, to // 2], recv_sem=f_rsem.at[i, to // 2],
            device_id=opposite, device_id_type=MESH,
        )

    is_first, is_last = q == 0, q == 15

    def relay(i):
        for edge, up in ((is_first, True), (is_last, False)):

            @pl.when(edge)
            def _():
                f_copy(i, up).wait_recv()
                relay_copy(i, up).start()

    for edge, to in ((is_first, 0), (is_last, 2)):

        @pl.when(edge)
        def _():
            for which in (0, 1):
                kv[which, to, :, pl.ds(KVC, KVC)] = jnp.zeros((FR, KVC), jnp.bfloat16)

    def neighbours(act_up, act_down, up_edge, down_edge):
        pl.when(jnp.logical_not(up_edge))(act_up)
        pl.when(jnp.logical_not(down_edge))(act_down)

    pl.semaphore_wait(barrier, 38)
    for i in range(4):
        k_copy(i).start()
    for i in range(4):
        k_copy(i).wait_recv()
        neighbours(lambda: f_copy(i, True).start(), lambda: f_copy(i, False).start(), is_last, is_first)
        if 1 <= i <= RELAYED:
            relay(i - 1)

    w_swap = [
        pltpu.make_async_remote_copy(
            src_ref=hbm.at[1 - c], dst_ref=vmem.at[pl.ds(FS, FS)], send_sem=wx_ssem.at[i], recv_sem=wx_rsem.at[i],
            device_id=sibling, device_id_type=MESH,
        )
        for i, (hbm, vmem) in enumerate(((w_in_hbm, win), (w_out_hbm, wout)))
    ]
    for cp in w_swap:
        cp.start()

    for cp in inputs:
        cp.wait()
    first = first_ref[0, 0] - (q - 1) * FR
    frame = lax.broadcasted_iota(jnp.int32, (WIN, 3 * FR), 1)
    row = lax.broadcasted_iota(jnp.int32, (WIN, 3 * FR), 0)
    band = jnp.where(frame == row + first, 1.0, 0.0).astype(jnp.bfloat16)
    squares = jnp.zeros((TOK, DH), jnp.float32)
    for part in (0, 1):
        for i in (2 * part, 2 * part + 1):
            neighbours(
                lambda: f_copy(i, True).wait_recv(), lambda: f_copy(i, False).wait_recv(), is_first, is_last
            )
        part_cols = pl.ds(part * KVC, KVC)
        keys, values = (
            dot(band, kv[which, :, :, part_cols].reshape(3 * FR, KVC)).astype(jnp.bfloat16) for which in (0, 1)
        )
        for h in range(KV_HEADS // 2):
            at = slice(h * DH, (h + 1) * DH)
            heads = [pl.ds(((part * 4 + h) * GROUP + g) * DH, DH) for g in range(GROUP)]
            rows = jnp.concatenate([queries_ref[:, cols] for cols in heads], axis=0)
            scores = lax.dot_general(
                rows, keys[:, at], (((1,), (1,)), ((), ())), preferred_element_type=jnp.float32
            ) * (1.0 / math.sqrt(DH))
            weights = jnp.exp(scores - jnp.max(scores, axis=1, keepdims=True))
            total = jnp.sum(weights, axis=1, keepdims=True)
            context = dot(weights.astype(jnp.bfloat16), values[:, at]) / total
            for g, cols in enumerate(heads):
                state = dec_ref[:, cols].astype(jnp.float32) + context[g * TOK : (g + 1) * TOK]
                state_ref[:, cols] = state
                squares += state * state
    inverse = lax.rsqrt(jnp.sum(squares, axis=1, keepdims=True) * (1.0 / D) + 1e-06)
    for h in range(HEADS):
        cols = pl.ds(h * DH, DH)
        normed_ref[:, cols] = (state_ref[:, cols] * inverse * gain_ref[:, cols]).astype(jnp.bfloat16)

    outgoing(0)
    a_start(0)

    own, mate = x * 2 + l, x * 2 + 1 - l

    def blk(x_, far=False):
        return x_ * 2 + (1 - l if far else l)

    gather = [
        (own, PP, across, mate),
        (own, QQ, right, blk(xl)),
        (own, QQ, left, blk(xr)),
        (own, PP, right, blk(xl)),
        (own, PP, left, blk(xr)),
        (own, QQ, across, mate),
        (mate, PP, right, blk(xl, True)),
        (mate, PP, left, blk(xr, True)),
        (blk(xl), QA, right, blk(xo)),
        (blk(xr), QB, left, blk(xo)),
        (blk(xl), QQ, across, blk(xl, True)),
        (blk(xr), QQ, across, blk(xr, True)),
        (blk(xl), PA, right, blk(xo)),
        (blk(xr), PB, left, blk(xo)),
        (blk(xl, True), PA, right, blk(xo, True)),
        (blk(xr, True), PB, left, blk(xo, True)),
        (blk(xo), QA, across, blk(xo, True)),
        (blk(xo), QB, across, blk(xo, True)),
    ]

    def wide(u, cols):
        return pl.ds((u % 2) * SIDE + cols[0], cols[1])

    def g_copy(u, i, received=False):
        sent, cols, there, got = gather[i]
        ref = xg.at[u // 2, got if received else sent, :, wide(u, cols)]
        return pltpu.make_async_remote_copy(
            src_ref=ref, dst_ref=ref, send_sem=g_ssem.at[u, i], recv_sem=g_rsem.at[u, i],
            device_id=there, device_id_type=MESH,
        )

    def g_start(wave, *which):
        for i in which:
            g_copy(wave, i).start()

    def g_wait(wave, *which):
        for i in which:
            g_copy(wave, i, True).wait_recv()

    def arrive(u):
        if u < 2:
            self_a[u].wait()
        each_peer(u, lambda d: a_recv(u, d).wait_recv())
        rows = dot(unpack_ref[...], in_msg[u].reshape(PEERS * MSG, SEG)).astype(jnp.bfloat16)
        for g in range(SEGS):
            xg[u // 2, own, :, wide(u, (g * SEG, SEG))] = rows[g * HALF : (g + 1) * HALF]

    def gather_1(wave):
        g_start(wave, 0, 1, 2, 3, 4, 5)

    def hand_on(u, received, then):
        g_wait(u, *received)
        g_start(u, *then)

    def gather_4(wave):
        g_wait(wave, 5, 10, 11, 12, 13, 14, 15, 16, 17)

    def hidden(u):
        rows = xg[u // 2, :, :, wide(u, (0, SIDE))].reshape(8 * HALF, SIDE)
        units = lax.dot_general(
            rows, win[:, wide(u, (0, SIDE))], (((1,), (1,)), ((), ())), preferred_element_type=jnp.float32
        )
        if u % 2 == 0:
            acc[...] = units
        else:
            hid[...] = jnp.maximum(acc[...] + units, 0.0).astype(jnp.bfloat16)

    def partial(u):
        for cols in (PA, QQ, PB):
            part = dot(hid[...], wout[:, wide(u, cols)])
            pt[u // 2, :, :, wide(u, cols)] = part.astype(jnp.bfloat16).reshape(8, HALF, cols[1])

    def span(home, cols):
        return lambda u: pt.at[u // 2, home, :, wide(u, cols)]

    def inner(buf, i, cols):
        return lambda u: buf.at[u, i, :, pl.ds(*cols)]

    sums = []
    for f in (1, 0):
        far = f == 1
        sums += [
            (span(blk(xo, far), PA), inner(r_p2r, f, PA), left),
            (span(blk(xo, far), PB), inner(r_p2l, f, (0, PB[1])), right),
            (span(blk(xl, far), PB), inner(r_pr, f, PB), left),
            (span(blk(xr, far), PA), inner(r_pl, f, PA), right),
            (span(blk(xl, far), PA), inner(r_pr, f, PA), left),
            (span(blk(xr, far), PB), inner(r_pl, f, PB), right),
        ]
    q0, q1 = (0, QA[1]), (QA[1], QB[1])
    sums += [
        (span(mate, PP), inner(r_py, 0, PP), across),
        (span(blk(xo, True), QQ), inner(r_qy, 0, (0, QQ[1])), across),
        (span(blk(xl, True), QQ), inner(r_qy, 1, (0, QQ[1])), across),
        (span(blk(xr, True), QQ), inner(r_qy, 2, (0, QQ[1])), across),
        (span(mate, QQ), inner(r_qy, 3, (0, QQ[1])), across),
        (span(blk(xo), QA), inner(r_q2r, 0, q0), left),
        (span(blk(xo), QB), inner(r_q2l, 0, (0, QB[1])), right),
        (span(blk(xl), QB), inner(r_qr, 0, q1), left),
        (span(blk(xr), QA), inner(r_ql, 0, q0), right),
        (span(blk(xl), QA), inner(r_qr, 0, q0), left),
        (span(blk(xr), QB), inner(r_ql, 0, q1), right),
    ]

    def s_copy(wave, i):
        src, dst, there = sums[i]
        return pltpu.make_async_remote_copy(
            src_ref=src(wave), dst_ref=dst(wave), send_sem=s_ssem.at[wave, i], recv_sem=s_rsem.at[wave, i],
            device_id=there, device_id_type=MESH,
        )

    def s_start(wave, *which):
        for i in which:
            s_copy(wave, i).start()

    def s_wait(wave, *which):
        for i in which:
            s_copy(wave, i).wait_recv()

    def add(u, home, cols, *terms):
        step = 128

        @pl.loop(0, cols[1] // step)
        def _(i):
            here = pl.ds(pl.multiple_of((u % 2) * SIDE + cols[0] + i * step, 128), step)
            total = pt[u // 2, home, :, here].astype(jnp.float32)
            for buf, j in terms:
                total += buf[u, j, :, pl.ds(pl.multiple_of(i * step, 128), step)].astype(jnp.float32)
            pt[u // 2, home, :, here] = total.astype(jnp.bfloat16)

    def sum_p2(u, f):
        n, far = (0, True) if f == 1 else (6, False)
        s_wait(u, n, n + 1)
        add(u, blk(xl, far), PA, (r_p2r, f))
        s_start(u, n + 4)
        add(u, blk(xr, far), PB, (r_p2l, f))
        s_start(u, n + 5)

    def sum_p1(u, f):
        n, far = (0, True) if f == 1 else (6, False)
        s_wait(u, n + 2, n + 3, n + 4, n + 5)
        add(u, blk(x, far), PP, (r_pr, f), (r_pl, f))
        if far:
            s_start(u, 12)

    def sum_py(u):
        s_wait(u, 12)
        add(u, own, PP, (r_py, 0))

    def sum_qy(u, i):
        s_wait(u, 13 + i)
        add(u, blk((xo, xl, xr)[i]), QQ, (r_qy, i))
        s_start(u, *((17, 18), (19,), (20,))[i])

    def sum_q2(u):
        s_wait(u, 17, 18)
        add(u, blk(xl), QA, (r_q2r, 0))
        s_start(u, 21)
        add(u, blk(xr), QB, (r_q2l, 0))
        s_start(u, 22)

    def sum_q1(u):
        s_wait(u, 16, 19, 20, 21, 22)
        add(u, own, QQ, (r_qy, 3), (r_qr, 0), (r_ql, 0))

    def send_back(u):
        ret_msg[u] = pack(pt[u // 2, own, :, wide(u, (0, SIDE))]).reshape(PEERS, MSG, SEG)
        each_peer(u, lambda d: b_copy(u, d).start())
        if u < 2:
            self_b[u].start()

    def come_back(u):
        if u < 2:
            self_b[u].wait()
        each_peer(u, lambda d: b_recv(u, d).wait_recv())
        wave = u // 2
        rows = dot(unpack_ref[...], ret_in[u].reshape(PEERS * MSG, SEG)).astype(jnp.bfloat16)
        for g in range(SEGS):
            cols = wide(u, (g * SEG, SEG))
            expert_out = dot(perm_t[:, wave * HALF : (wave + 1) * HALF], rows[g * HALF : (g + 1) * HALF])
            mixed = state_ref[:, cols] + scale * expert_out
            if wave == 0:
                state_ref[:, cols] = mixed
            else:
                out_ref[0, :, cols] = mixed.astype(jnp.bfloat16)

    def sums_start(u):
        s_start(u, 0, 6, 1, 7, 13, 14, 15, 16, 3, 9, 2, 8)

    def sent(u, *kinds):
        for kind in kinds:
            if kind == "a":
                each_peer(u, lambda d: a_recv(u, d).wait_send())
            if kind == "g":
                for i in range(len(gather)):
                    g_copy(u, i).wait_send()
            if kind == "s":
                for i in range(len(sums)):
                    s_copy(u, i).wait_send()
            if kind == "b":
                each_peer(u, lambda d: b_recv(u, d).wait_send())

    a_start(1)
    outgoing(1)
    arrive(0)
    gather_1(0)
    a_start(2)
    arrive(1)
    gather_1(1)
    a_start(3)
    hand_on(0, (0,), (6, 7))
    hand_on(0, (1, 2), (8, 9, 10, 11))
    hand_on(0, (3, 4), (12, 13))
    arrive(2)
    gather_1(2)
    hand_on(1, (0,), (6, 7))
    hand_on(1, (1, 2), (8, 9, 10, 11))
    hand_on(1, (3, 4), (12, 13))
    arrive(3)
    hand_on(0, (6, 7), (14, 15))
    gather_1(3)
    hand_on(0, (8, 9), (16, 17))
    hand_on(2, (0,), (6, 7))
    hand_on(2, (1, 2), (8, 9, 10, 11))
    hand_on(2, (3, 4), (12, 13))
    hand_on(1, (6, 7), (14, 15))
    hand_on(1, (8, 9), (16, 17))
    hand_on(3, (0,), (6, 7))
    hand_on(3, (1, 2), (8, 9, 10, 11))
    gather_4(0)
    for cp in w_local:
        cp.wait()
    for cp in w_swap:
        cp.wait_recv()
    hidden(0)
    hand_on(3, (3, 4), (12, 13))
    hand_on(2, (6, 7), (14, 15))
    hand_on(2, (8, 9), (16, 17))
    gather_4(1)
    hidden(1)
    partial(0)
    sums_start(0)
    hand_on(3, (6, 7), (14, 15))
    partial(1)
    hand_on(3, (8, 9), (16, 17))
    sums_start(1)
    gather_4(2)
    hidden(2)
    sum_qy(0, 0)
    sum_p2(0, 1)
    sum_p2(0, 0)
    sum_qy(0, 1)
    sum_qy(0, 2)
    sum_p2(1, 1)
    sum_p2(1, 0)
    gather_4(3)
    hidden(3)
    partial(3)
    sum_q2(0)
    sum_qy(1, 0)
    sum_p1(0, 1)
    partial(2)
    sums_start(2)
    sum_qy(1, 2)
    sum_qy(1, 1)
    sum_p1(1, 1)
    sum_p1(0, 0)
    sum_p1(1, 0)
    sum_q1(0)
    sum_py(0)
    send_back(0)
    sum_p2(2, 1)
    sum_qy(2, 0)
    sum_q2(1)
    sums_start(3)
    sum_qy(2, 1)
    sum_p2(2, 0)
    sent(0, "a", "g")
    sum_qy(2, 2)
    sum_p1(2, 1)
    sum_q2(2)
    come_back(0)
    sum_py(1)
    sum_p2(3, 1)
    sum_q1(1)
    sum_qy(3, 0)
    send_back(1)
    sum_qy(3, 1)
    sent(1, "a", "g")
    sum_p2(3, 0)
    sum_qy(3, 2)
    sum_p1(2, 0)
    sum_q1(2)
    sum_p1(3, 1)
    sum_q2(3)
    sum_py(2)
    send_back(2)
    sum_p1(3, 0)
    sent(2, "a", "g")
    sum_py(3)
    sum_q1(3)
    send_back(3)
    come_back(1)
    sent(3, "a", "g")
    come_back(2)
    come_back(3)
    for u in range(UNITS):
        sent(u, "s", "b")

    for i in range(4):
        k_copy(i).wait_send()
        neighbours(lambda: f_copy(i, True).wait_send(), lambda: f_copy(i, False).wait_send(), is_last, is_first)
        if i < RELAYED:
            pl.when(is_first)(lambda: relay_copy(i, True).wait_send())
            pl.when(is_last)(lambda: relay_copy(i, False).wait_send())
    for cp in w_swap:
        cp.wait_send()


def body(
    queries, dec_state, enc_kv, band_start, norm_gain, route_ids, keep, route_prob, w_in, w_out
):
    order = message_order()
    vmem = pl.BlockSpec(memory_space=pltpu.VMEM)
    hbm = pl.BlockSpec(memory_space=pl.ANY)
    bf = jnp.bfloat16
    return pl.pallas_call(
        moe_kernel,
        out_shape=jax.ShapeDtypeStruct((1, TOK, D), bf),
        in_specs=[pl.BlockSpec(memory_space=pltpu.SMEM)] + [vmem] * 4 + [hbm] * 7,
        out_specs=vmem,
        scratch_shapes=[
            pltpu.VMEM((SEGS * HALF, SEGS * HALF), bf),
            pltpu.VMEM((SEGS * HALF, SEGS * HALF), bf),
            pltpu.VMEM((TOK, D), bf),
            pltpu.VMEM((TOK, D), bf),
            pltpu.VMEM((TOK, D), jnp.float32),
            pltpu.VMEM((TOK, D), bf),
            pltpu.VMEM((2, 3, FR, KV_HEADS * DH), bf),
            pltpu.SemaphoreType.DMA((4,)),
            pltpu.SemaphoreType.DMA((4,)),
            pltpu.SemaphoreType.DMA((4,)),
            pltpu.SemaphoreType.DMA((4, 2)),
            pltpu.SemaphoreType.DMA((4, 2)),
            pltpu.SemaphoreType.DMA((2, 2)),
            pltpu.VMEM((2 * FS, D), bf),
            pltpu.VMEM((2 * FS, D), bf),
            pltpu.VMEM((8 * HALF, 2 * FS), jnp.float32),
            pltpu.VMEM((8 * HALF, 2 * FS), bf),
            pltpu.VMEM((2, 8, HALF, D), bf),
            pltpu.VMEM((2, 8, HALF, D), bf),
            pltpu.VMEM((UNITS, PEERS, MSG, SEG), bf),
            pltpu.VMEM((UNITS, PEERS, MSG, SEG), bf),
            pltpu.VMEM((UNITS, PEERS, MSG, SEG), bf),
            pltpu.VMEM((UNITS, PEERS, MSG, SEG), bf),
            pltpu.VMEM((UNITS, 2, HALF, PA[1]), bf),
            pltpu.VMEM((UNITS, 2, HALF, PB[1]), bf),
            pltpu.VMEM((UNITS, 2, HALF, PP[1]), bf),
            pltpu.VMEM((UNITS, 2, HALF, PP[1]), bf),
            pltpu.VMEM((UNITS, 1, HALF, PP[1]), bf),
            pltpu.VMEM((UNITS, 4, HALF, QQ[1]), bf),
            pltpu.VMEM((UNITS, 1, HALF, QA[1]), bf),
            pltpu.VMEM((UNITS, 1, HALF, QB[1]), bf),
            pltpu.VMEM((UNITS, 1, HALF, QQ[1]), bf),
            pltpu.VMEM((UNITS, 1, HALF, QQ[1]), bf),
            pltpu.SemaphoreType.DMA((2,)),
            pltpu.SemaphoreType.DMA((2,)),
            pltpu.SemaphoreType.DMA((2,)),
            pltpu.SemaphoreType.DMA((UNITS, PEERS)),
            pltpu.SemaphoreType.DMA((UNITS, PEERS)),
            pltpu.SemaphoreType.DMA((UNITS, PEERS)),
            pltpu.SemaphoreType.DMA((UNITS, PEERS)),
            pltpu.SemaphoreType.DMA((4,)),
            pltpu.SemaphoreType.DMA((UNITS, 18)),
            pltpu.SemaphoreType.DMA((UNITS, 18)),
            pltpu.SemaphoreType.DMA((UNITS, 23)),
            pltpu.SemaphoreType.DMA((UNITS, 23)),
        ],
        compiler_params=pltpu.CompilerParams(
            collective_id=0, has_side_effects=True, vmem_limit_bytes=60 * 2**20
        ),
    )(
        band_start,
        route_ids.reshape(1, TOK),
        keep,
        route_prob,
        norm_gain.reshape(1, D),
        jnp.asarray(order, bf),
        jnp.asarray(order.T, bf),
        queries,
        dec_state,
        enc_kv,
        w_in,
        w_out,
    )


def solution(mesh):
    return jax.shard_map(
        body,
        mesh=mesh,
        in_specs=(
            P(("section", "expert"), "seq", None),
            P(("section", "expert"), "seq", None),
            P(None, ("section", "expert"), "seq", None),
            P(("section", "expert"), "seq"),
            P(),
            P(("section", "expert"), "seq", None),
            P(("section", "expert"), "seq"),
            P(("section", "expert"), "seq"),
            P("seq", ("section", "expert"), None),
            P("seq", ("section", "expert"), None),
        ),
        out_specs=P(("section", "expert"), "seq", None),
        check_vma=False,
    )
```
